32 devices in a mesh: fibre: 2 (over y), chan: 4 (over z), win: 2 (over x), grp: 2 (over core).
Axes of the slice: x: 2, y: 2, z: 4, core: 2. Of those that a mesh axis runs over, the one named last changes fastest.
Arguments:
- file_rows: bfloat16 [1280, 8192], P(('fibre', 'chan'), 'win'), parts along dimension 0, may hold values from -150 to 150
- channel_list: int32 [1280], P(('fibre', 'chan')), parts along dimension 0, may hold values from 0 to 512, as said below
- filter_taps: bfloat16 [64], replicated, may hold values from -0.75 to 0.75
- source_channels: int32 [8, 64], P(('fibre', 'grp')), parts along dimension 0, may hold values from 0 to 511, as said below
Outputs:
- correlations: float32 [1024, 256, 256], P(('fibre', 'chan', 'win'), 'grp'), parts along dimension 0
The draws below stay inside these ranges and needn't reach their ends.
There are 2 independent parts, one for each index of `fibre`. The reference program is written for one: setup_inputs(seed, part) draws one part's arguments, and reference() takes and returns one part's arrays. A program takes and returns all parts, laid end to end along the dimension named above; an argument that names none is the same for every part. Nothing has to cross between parts.
Inputs may be any that keep to these rules, and one draw needn't show every extreme that they name: `channel_list`: the rows of one device are the 160 consecutive rows d * 160 on; its rows that hold data come first. Every channel appears exactly once over all devices; of one device's rows at most 32 lie in one block of channels b * 128 to (b + 1) * 128 - 1, and some device reaches 32 in every block; every device has rows without data. `source_channels`: all 256 channels are different.
All inputs are finite; a program needn't handle non-finite values.
Results may differ from the reference program's by a relative error of at most 0.0076.
Values may be sent and summed in bfloat16 or wider, within the bound.
A program may use at most 128 MiB of HBM per device.

```python
import math
import jax
import jax.numpy as jnp
from jax import lax

L = 4096
FB = 256
F0 = 8
LAGS = 256
TAPS = 64
HALF = 64
SMOOTH = 8
SRC_GRP = 64
CH_DEV = 128
SLOT = 32
ROWCAP = 160
CHANNELS = 512
GROUPS = 4
SOURCES = 256
WINDOWS = 2
SAMPLES = 8192


def ingest_layout(key):
    chan_count = CHANNELS // CH_DEV
    key_order, key_fill, key_shuffle = jax.random.split(jax.random.fold_in(key, 11), 3)
    order = jax.random.permutation(key_order, chan_count)
    owners = jnp.arange(chan_count, dtype=jnp.int32)
    others = 1 + jnp.mod(3 * owners[:, None] + jnp.arange(3, dtype=jnp.int32)[None, :], chan_count - 1)
    ranks = jnp.concatenate([jnp.zeros((chan_count, 1), jnp.int32), others], axis=1)
    senders = order[ranks]
    owner_keys = jax.random.split(key_fill, chan_count)
    within = jax.vmap(lambda one_key: jax.random.permutation(one_key, CH_DEV))(owner_keys)
    channel = owners[:, None] * CH_DEV + within
    sender_of = jnp.repeat(senders, SLOT, axis=1)
    flat_sender = sender_of.reshape(-1).astype(jnp.int32)
    flat_channel = channel.reshape(-1).astype(jnp.int32)
    ties = jax.random.permutation(key_shuffle, CHANNELS).astype(jnp.int32)
    order_index = jnp.argsort(flat_sender * CHANNELS + ties, stable=True)
    sorted_sender = flat_sender[order_index]
    sorted_channel = flat_channel[order_index]
    counts = jnp.sum((flat_sender[:, None] == owners[None, :]).astype(jnp.int32), axis=0)
    starts = jnp.cumsum(counts) - counts
    position = jnp.arange(CHANNELS, dtype=jnp.int32) - starts[sorted_sender]
    empty = jnp.full((chan_count, ROWCAP), CHANNELS, jnp.int32)
    table = empty.at[sorted_sender, position].set(sorted_channel)
    return table.reshape(-1).astype(jnp.int32)


def draw_channel_list(key, part):
    return ingest_layout(key)


def draw_source_channels(key, part):
    key_pick, key_mix = jax.random.split(jax.random.fold_in(key, 23))
    middle = 1 + jax.random.permutation(key_pick, CHANNELS - 2)[:SOURCES - 2]
    picks = jnp.concatenate([jnp.array([0, CHANNELS - 1], jnp.int32), middle.astype(jnp.int32)])
    return jax.random.permutation(key_mix, picks).reshape(GROUPS, SRC_GRP).astype(jnp.int32)


def draw_file_rows(key, part):
    key_base, key_env = jax.random.split(jax.random.fold_in(key, 31), 2)
    total_rows = ROWCAP * (CHANNELS // CH_DEV)
    values = jnp.clip(jax.random.normal(key_base, (total_rows, SAMPLES), jnp.float32), -5.0, 5.0)
    envelope = jnp.exp(jax.random.uniform(key_env, (total_rows, SAMPLES // 16, 1), jnp.float32, 0.0, math.log(10.0)))
    shaped = values.reshape(total_rows, SAMPLES // 16, 16) * envelope
    return shaped.reshape(total_rows, SAMPLES).astype(jnp.bfloat16)


def centred(rng, dims, width, bound, kind=jnp.bfloat16):
    values = jax.random.normal(rng, dims, jnp.float32) * width
    return jnp.minimum(jnp.maximum(values, -bound), bound).astype(kind)


def setup_inputs(seed: int = 0, part: int = 0) -> dict:
    key_of = jax.random.split(jax.random.key(seed), 5)
    part_splits = jax.random.split(jax.random.fold_in(key_of[4], part), 5)
    return {
        "file_rows": draw_file_rows(jax.random.fold_in(jax.random.fold_in(key_of[4], part), 71), part),
        "channel_list": draw_channel_list(jax.random.fold_in(jax.random.fold_in(key_of[4], part), 71), part),
        "filter_taps": centred(key_of[2], (TAPS,), TAPS ** -0.5, 0.75),
        "source_channels": draw_source_channels(jax.random.fold_in(jax.random.fold_in(key_of[4], part), 71), part),
    }


epsilon = 1e-06
water_level = 0.1

def make_tables():
    samples = jnp.arange(L, dtype=jnp.int32)
    bins = jnp.arange(FB, dtype=jnp.int32) + F0
    phase = jnp.mod(samples[:, None] * bins[None, :], L).astype(jnp.float32) * (2.0 * math.pi / L)
    forward = jnp.concatenate([jnp.cos(phase), -jnp.sin(phase)], axis=1).astype(jnp.bfloat16)
    shifts = jnp.arange(LAGS, dtype=jnp.int32) - LAGS // 2
    turn = jnp.mod(bins[:, None] * shifts[None, :], L).astype(jnp.float32) * (2.0 * math.pi / L)
    inverse = (jnp.concatenate([jnp.cos(turn), -jnp.sin(turn)], axis=0) / math.sqrt(FB)).astype(jnp.bfloat16)
    offsets = jnp.arange(FB, dtype=jnp.int32)
    smoother = (jnp.abs(offsets[:, None] - offsets[None, :]) <= SMOOTH).astype(jnp.float32)
    return (forward, inverse, smoother)

def whiten(window_rows, filter_taps, forward, smoother):
    kernel = filter_taps[::-1].reshape(1, 1, TAPS)
    filtered = lax.conv_general_dilated(window_rows[:, None, :], kernel, (1,), [(TAPS - 1, 0)], dimension_numbers=('NCH', 'OIH', 'NCH'), preferred_element_type=jnp.float32)[:, 0, :]
    magnitude_sum = lax.reduce_window(jnp.abs(filtered), jnp.zeros((), filtered.dtype), lax.add, (1, 2 * HALF + 1), (1, 1), ((0, 0), (HALF, HALF)))
    position = jnp.arange(L, dtype=jnp.int32)
    counts = (jnp.minimum(position, HALF) + jnp.minimum(L - 1 - position, HALF) + 1).astype(jnp.float32)
    normalized = (filtered / (magnitude_sum / counts + epsilon)).astype(jnp.bfloat16)
    spectrum = jnp.dot(normalized, forward, preferred_element_type=jnp.float32)
    real_part = spectrum[:, :FB]
    imag_part = spectrum[:, FB:]
    energy = real_part * real_part + imag_part * imag_part
    smooth = jnp.dot(energy, smoother, precision=lax.Precision.HIGHEST, preferred_element_type=jnp.float32) / lax.optimization_barrier(jnp.sum(smoother, axis=0))
    average = lax.optimization_barrier(jnp.mean(energy, axis=1, keepdims=True))
    factor = lax.rsqrt(smooth + water_level * average + epsilon)
    return (spectrum * jnp.concatenate([factor, factor], axis=1)).astype(jnp.bfloat16)

def correlate(chan_spec, src_spec, inverse):
    chan_real = chan_spec[:, :, :FB].astype(jnp.float32)[:, None]
    chan_imag = chan_spec[:, :, FB:].astype(jnp.float32)[:, None]
    src_real = src_spec[:, :, :FB].astype(jnp.float32)[None]
    src_imag = src_spec[:, :, FB:].astype(jnp.float32)[None]
    product = jnp.concatenate([chan_real * src_real + chan_imag * src_imag, chan_imag * src_real - chan_real * src_imag], axis=-1).astype(jnp.bfloat16)
    channels = chan_spec.shape[0]
    sources = src_spec.shape[0]
    windows = chan_spec.shape[1]
    stacked = product.reshape(channels * sources, windows * 2 * FB)
    result = jnp.dot(stacked, jnp.tile(inverse, (windows, 1)), preferred_element_type=jnp.float32)
    return result.reshape(channels, sources, LAGS)

def reference(file_rows, channel_list, filter_taps, source_channels):
    forward, inverse, smoother = make_tables()
    usable = channel_list < CHANNELS
    target = jnp.where(usable, channel_list, CHANNELS).astype(jnp.int32)
    traces = jnp.zeros((CHANNELS, SAMPLES), jnp.bfloat16).at[target].set(file_rows, mode='drop')
    whitened = whiten(traces.reshape(CHANNELS * WINDOWS, L), filter_taps, forward, smoother)
    whitened = whitened.reshape(CHANNELS, WINDOWS, 2 * FB)
    source_spectra = whitened[source_channels.reshape(-1)]
    blocks = whitened.reshape(CHANNELS // SLOT, SLOT, WINDOWS, 2 * FB)
    result = lax.map(lambda block_rows: correlate(block_rows, source_spectra, inverse), blocks)
    return result.reshape(CHANNELS, SOURCES, LAGS)
```

```python
import functools
import math

import jax
import jax.numpy as jnp
import ml_dtypes
import numpy as np
from jax import lax
from jax.experimental import pallas as pl
from jax.experimental.pallas import tpu as pltpu
from jax.sharding import PartitionSpec as P

L = 4096
FB = 256
F0 = 8
LAGS = 256
TAPS = 64
HALF = 64
SMOOTH = 8
CH_DEV = 128
FOLD = 4
CHUNK = 256
SPECTRA_VMEM = 52 * 1024 * 1024
CORRELATE_VMEM = 40 * 1024 * 1024

epsilon = 1e-06
water_level = 0.1


def quarter_table():
    samples = np.arange(L // FOLD)
    bins = np.arange(FB) + F0
    phase = np.mod(samples[:, None] * bins[None, :], L) * (2.0 * math.pi / L)
    table = np.concatenate([np.cos(phase), -np.sin(phase)], axis=1)
    return table.astype(np.float32).astype(ml_dtypes.bfloat16)


def inverse_table():
    bins = np.arange(FB) + F0
    shifts = np.arange(LAGS) - LAGS // 2
    turn = np.mod(bins[:, None] * shifts[None, :], L).astype(np.float32) * np.float32(2.0 * math.pi / L)
    inverse = np.concatenate([np.cos(turn), -np.sin(turn)], axis=0) / math.sqrt(FB)
    return inverse.astype(ml_dtypes.bfloat16)


def dot(a, b):
    return jnp.dot(a, b, preferred_element_type=jnp.float32)


def iota(shape, axis):
    return lax.broadcasted_iota(jnp.int32, shape, axis)


def other(index, step):
    for bit in range(step.bit_length()):
        if (step >> bit) & 1:
            index = index + 2**bit - 2 ** (bit + 1) * ((index // 2**bit) % 2)
    return index


def build_toeplitz(taps_ref, wide_taps, toeplitz):
    wide_taps[...] = jnp.zeros_like(wide_taps)
    wide_taps[:, :TAPS] = taps_ref[...].astype(jnp.float32)
    moved = jnp.broadcast_to(wide_taps[...], (128, 256))
    row = iota((128, 256), 0)
    for bit in range(7):
        moved = jnp.where((row >> bit) & 1 == 1, pltpu.roll(moved, 2**bit, 1), moved)
    moved = moved.astype(jnp.bfloat16)
    here, before = moved[:, :128], moved[:, 128:]
    zero = jnp.zeros((128, 128), jnp.bfloat16)
    toeplitz[0:128, :] = jnp.concatenate([before, zero], axis=1)
    toeplitz[128:256, :] = jnp.concatenate([here, before], axis=1)
    toeplitz[256:384, :] = jnp.concatenate([zero, here], axis=1)


def whiten_rows(rows_ref, toeplitz, filt, size, normed, table, table_ready):
    count = rows_ref.shape[0]
    blocks = L // CHUNK
    group = 4
    zero = jnp.zeros((count, 128), jnp.bfloat16)
    for g in range(0, blocks, group):
        parts = [
            rows_ref[:, j * CHUNK - 128 : (j + 1) * CHUNK]
            if j
            else jnp.concatenate([zero, rows_ref[:, :CHUNK]], axis=1)
            for j in range(g, g + group)
        ]
        part = dot(jnp.concatenate(parts, axis=0), toeplitz[...])
        filt[g * count : (g + group) * count, :] = part
        size[g * count : (g + group) * count, :] = jnp.abs(part).astype(jnp.bfloat16)

    reach = jnp.abs(iota((512, CHUNK), 0) - 128 - iota((512, CHUNK), 1)) <= HALF
    band = reach.astype(jnp.float32).astype(jnp.bfloat16)
    for g in range(0, blocks, group):
        parts = []
        for j in range(g, g + group):
            low = size[(j - 1) * count : j * count, 128:] if j else zero
            high = size[(j + 1) * count : (j + 2) * count, :128] if j < blocks - 1 else zero
            parts.append(jnp.concatenate([low, size[j * count : (j + 1) * count, :], high], axis=1))
        total = dot(jnp.concatenate(parts, axis=0), band)
        for j in range(g, g + group):
            position = j * CHUNK + iota((1, CHUNK), 1)
            width = jnp.minimum(position, HALF) + jnp.minimum(L - 1 - position, HALF) + 1
            scale = 1.0 / width.astype(jnp.float32)
            fold, at = divmod(j * CHUNK, L // FOLD)
            normed[fold * count : (fold + 1) * count, at : at + CHUNK] = (
                filt[j * count : (j + 1) * count, :]
                / (total[(j - g) * count : (j - g + 1) * count] * scale + epsilon)
            ).astype(jnp.bfloat16)

    table_ready()
    quarters = dot(normed[...], table[...])
    k = iota((1, FB), 1) + F0
    real = imag = jnp.zeros((count, FB), jnp.float32)
    for fold in range(FOLD):
        turns = (k * fold) % 4
        cosine = jnp.where(turns == 0, 1.0, jnp.where(turns == 2, -1.0, 0.0))
        sine = jnp.where(turns == 1, 1.0, jnp.where(turns == 3, -1.0, 0.0))
        re = quarters[fold * count : (fold + 1) * count, :FB]
        im = quarters[fold * count : (fold + 1) * count, FB:]
        real = real + cosine * re + sine * im
        imag = imag + cosine * im - sine * re
    energy = real * real + imag * imag
    near = jnp.abs(iota((FB, FB), 0) - iota((FB, FB), 1)) <= SMOOTH
    near = near.astype(jnp.float32).astype(jnp.bfloat16)
    upper = energy.astype(jnp.bfloat16)
    left = energy - upper.astype(jnp.float32)
    middle = left.astype(jnp.bfloat16)
    lower = (left - middle.astype(jnp.float32)).astype(jnp.bfloat16)
    split = dot(jnp.concatenate([upper, middle, lower], axis=0), near)
    total = split[:count] + split[count : 2 * count] + split[2 * count :]
    k = iota((1, FB), 1)
    width = jnp.minimum(k, SMOOTH) + jnp.minimum(FB - 1 - k, SMOOTH) + 1
    smooth = total / width.astype(jnp.float32)
    level = jnp.sum(energy, axis=1, keepdims=True) * (1.0 / FB)
    factor = lax.rsqrt(smooth + water_level * level + epsilon)
    return real * factor, imag * factor


def spectra_kernel(sizes, taps_hbm, sources_hbm, label_hbm, file_ref, table_ref, turn_ref, chan_ref, src_ref, inverse_ref,
                   taps_ref, sources_ref, label_ref, rows, filt, size, normed, toeplitz, wide_taps, table, held, labels,
                   load_sems, send_sems, recv_sems, label_sems):
    zs, xs, cs = sizes
    z, x, c = lax.axis_index("chan"), lax.axis_index("win"), lax.axis_index("grp")
    share = rows.shape[0]
    count = share * cs
    own = pl.ds(pl.multiple_of(c * share, share), share)

    fetch = pltpu.make_async_copy(file_ref.at[own, :], rows, load_sems.at[0])
    fetch.start()
    small = []
    for source, target in ((taps_hbm, taps_ref), (label_hbm, label_ref), (sources_hbm, sources_ref)):
        copy = pltpu.make_async_copy(source, target, load_sems.at[3 + len(small)])
        copy.start()
        small.append(copy)
    load = pltpu.make_async_copy(table_ref, table, load_sems.at[1])
    load.start()
    turn = pltpu.make_async_copy(turn_ref, inverse_ref, load_sems.at[2])
    turn.start()

    barrier = pltpu.get_barrier_semaphore()
    for axis, extent, index in (("chan", zs, z), ("win", xs, x), ("grp", cs, c)):
        for step in range(1, extent):
            pl.semaphore_signal(
                barrier, inc=1, device_id={axis: other(index, step)},
                device_id_type=pl.DeviceIdType.MESH,
            )

    labels[0] = jnp.zeros(labels.shape[1:], jnp.int32)
    for copy in small:
        copy.wait()
    labels[0, :, :count] = label_ref[:, :count]
    build_toeplitz(taps_ref, wide_taps, toeplitz)
    fetch.wait()
    real, imag = whiten_rows(rows, toeplitz, filt, size, normed, table, load.wait)
    held[0, 0, own, :FB] = real.astype(jnp.bfloat16)
    held[0, 0, own, FB:] = imag.astype(jnp.bfloat16)

    pl.semaphore_wait(barrier, zs + xs + cs - 3)

    copies = {}

    def send(d, e, f, source, target):
        copy = pltpu.make_async_remote_copy(
            src_ref=held.at[source[1], source[0], own],
            dst_ref=held.at[e, d, own],
            send_sem=send_sems.at[d, e, f],
            recv_sem=recv_sems.at[d, e, f],
            device_id=target,
            device_id_type=pl.DeviceIdType.MESH,
        )
        copy.start()
        copies[d, e, f] = copy

    def along_win(d):
        for e in range(1, xs):
            send(d, e, 0, (d, 0), {"win": other(x, e)})

    def along_chan(d, e):
        send(d, e, 0, (0, e), {"chan": other(z, d)})

    def along_grp(d, e):
        for f in range(1, cs):
            send(d, e, f, (d, e), {"grp": other(c, f)})

    across = zs - 1
    told = []
    for d in range(1, zs):
        copy = pltpu.make_async_remote_copy(
            src_ref=labels.at[0],
            dst_ref=labels.at[d],
            send_sem=label_sems.at[0, d],
            recv_sem=label_sems.at[1, d],
            device_id={"chan": other(z, d)},
            device_id_type=pl.DeviceIdType.MESH,
        )
        copy.start()
        told.append(copy)
    along_win(0)
    for d in range(1, zs):
        along_chan(d, 0)
    along_grp(0, 0)

    groups, width = sources_ref.shape
    channels = chan_ref.shape[0]
    diagonal = iota((width, width), 0) == iota((width, width), 1)
    wanted = [
        jnp.sum(jnp.where(diagonal, sources_ref[g : g + 1, :], 0), axis=1, keepdims=True)
        for g in range(groups)
    ]
    wanted.append(z * CH_DEV + x * channels + iota((channels, 1), 0))
    wanted = jnp.concatenate(wanted, axis=0)

    for e in range(1, xs):
        copies[0, e, 0].wait_recv()
        if across:
            along_chan(across, e)
        along_grp(0, e)
    for d in range(1, zs):
        copies[d, 0, 0].wait_recv()
        if d != across:
            along_win(d)
        along_grp(d, 0)

    for copy in told:
        copy.wait()
    span = max(1, 2 * FB // count)
    picks = []
    for d in range(0, zs, span):
        names = jnp.concatenate([labels[d + i, :, :count] for i in range(min(span, zs - d))], axis=1)
        picks.append((wanted == names).astype(jnp.float32).astype(jnp.bfloat16))

    def select(e):
        total = None
        for d, pick in zip(range(0, zs, span), picks):
            block = held[e, d : d + span]
            part = dot(pick, block.reshape(block.shape[0] * count, 2 * FB))
            total = part if total is None else total + part
        at = e * 2 * FB
        src_ref[:, at : at + 2 * FB] = total[: groups * width].astype(jnp.bfloat16)
        chan_ref[:, at : at + 2 * FB] = total[groups * width :]

    for d in range(zs):
        for f in range(1, cs):
            copies[d, 0, f].wait_recv()
    select(0)
    for e in range(1, xs):
        for d in range(1, zs):
            copies[d, e, 0].wait_recv()
            along_grp(d, e)
    for e in range(1, xs):
        for d in range(zs):
            for f in range(1, cs):
                copies[d, e, f].wait_recv()
        select(e)
    for copy in copies.values():
        copy.wait_send()
    turn.wait()


def correlate_kernel(wins, steps, inverse_ref, src_ref, chan_ref, out_ref, made, sems):
    inverse = inverse_ref[...]
    copies = []
    begin = 0
    for step in steps:
        for c in range(begin, begin + step):
            real = imag = None
            for w in range(wins):
                at = w * 2 * FB
                p, q = src_ref[:, at : at + FB], src_ref[:, at + FB : at + 2 * FB]
                row = chan_ref[c : c + 1, at : at + 2 * FB].astype(jnp.bfloat16)
                a, b = row[:, :FB], row[:, FB:]
                re, im = a * p + b * q, b * p - a * q
                real = re if real is None else real + re
                imag = im if imag is None else imag + im
            made[c] = dot(jnp.concatenate([real, imag], axis=1), inverse)
        part = pl.ds(begin, step)
        copy = pltpu.make_async_copy(made.at[part], out_ref.at[part], sems.at[len(copies)])
        copy.start()
        copies.append(copy)
        begin += step
    for copy in copies:
        copy.wait()


def local(file_rows, channel_list, filter_taps, source_channels):
    chan_count = lax.axis_size("chan")
    wins = lax.axis_size("win")
    cores = lax.axis_size("grp")
    count = chan_count * (CH_DEV // 4)
    share = count // cores
    channels = CH_DEV // wins
    groups, width = source_channels.shape
    sources = groups * width
    assert file_rows.shape[1] == L

    vmem = pl.BlockSpec(memory_space=pltpu.VMEM)
    hbm = pl.BlockSpec(memory_space=pltpu.HBM)
    given = (
        filter_taps.reshape(1, TAPS),
        source_channels,
        channel_list.reshape(1, -1),
        file_rows,
        jnp.asarray(quarter_table()),
        jnp.asarray(inverse_table()),
    )
    chan_spec, src_spec, inverse = pl.pallas_call(
        functools.partial(spectra_kernel, (chan_count, wins, cores)),
        in_specs=[hbm] * 6,
        out_specs=[vmem] * 3,
        out_shape=[
            pltpu.VMEM((channels, wins * 2 * FB), jnp.float32),
            pltpu.VMEM((sources, wins * 2 * FB), jnp.bfloat16),
            pltpu.VMEM((2 * FB, LAGS), jnp.bfloat16),
        ],
        scratch_shapes=[
            pltpu.VMEM((1, TAPS), jnp.bfloat16),
            pltpu.VMEM((groups, width), jnp.int32),
            pltpu.VMEM((1, channel_list.shape[0]), jnp.int32),
            pltpu.VMEM((share, L), jnp.bfloat16),
            pltpu.VMEM((L // CHUNK * share, CHUNK), jnp.float32),
            pltpu.VMEM((L // CHUNK * share, CHUNK), jnp.bfloat16),
            pltpu.VMEM((FOLD * share, L // FOLD), jnp.bfloat16),
            pltpu.VMEM((384, 256), jnp.bfloat16),
            pltpu.VMEM((1, 256), jnp.float32),
            pltpu.VMEM((L // FOLD, 2 * FB), jnp.bfloat16),
            pltpu.VMEM((wins, chan_count, count, 2 * FB), jnp.bfloat16),
            pltpu.VMEM((chan_count, 1, -(-count // 128) * 128), jnp.int32),
            pltpu.SemaphoreType.DMA((6,)),
            pltpu.SemaphoreType.DMA((chan_count, wins, cores)),
            pltpu.SemaphoreType.DMA((chan_count, wins, cores)),
            pltpu.SemaphoreType.DMA((2, chan_count)),
        ],
        compiler_params=pltpu.CompilerParams(
            collective_id=0, has_side_effects=True, vmem_limit_bytes=SPECTRA_VMEM
        ),
        name="spectra",
    )(*(pltpu.with_memory_space_constraint(array, pltpu.HBM) for array in given))

    step = min(8, channels // 2)
    edge = step // 2
    steps = (edge,) + (step,) * (channels // step - 1) + (edge,)
    return pl.pallas_call(
        functools.partial(correlate_kernel, wins, steps),
        in_specs=[vmem, vmem, vmem],
        out_specs=pl.BlockSpec(memory_space=pl.ANY),
        out_shape=jax.ShapeDtypeStruct((channels, sources, LAGS), jnp.float32),
        scratch_shapes=[
            pltpu.VMEM((channels, sources, LAGS), jnp.float32),
            pltpu.SemaphoreType.DMA((len(steps),)),
        ],
        compiler_params=pltpu.CompilerParams(vmem_limit_bytes=CORRELATE_VMEM),
        name="correlate",
    )(inverse, src_spec, chan_spec)


def solution(mesh):
    placed = (P(("fibre", "chan"), "win"), P(("fibre", "chan")), P(), P(("fibre", "grp"), None))
    return jax.shard_map(
        local,
        mesh=mesh,
        in_specs=placed,
        out_specs=P(("fibre", "chan", "win"), "grp", None),
        check_vma=False,
    )
```

```python
import functools
import math

import jax
import jax.numpy as jnp
import ml_dtypes
import numpy as np
from jax import lax
from jax.experimental import pallas as pl
from jax.experimental.pallas import tpu as pltpu
from jax.sharding import PartitionSpec as P

L = 4096
FB = 256
F0 = 8
LAGS = 256
TAPS = 64
HALF = 64
SMOOTH = 8
CH_DEV = 128
FOLD = 4
CHUNK = 256
SPECTRA_VMEM = 52 * 1024 * 1024
CORRELATE_VMEM = 40 * 1024 * 1024

epsilon = 1e-06
water_level = 0.1


def quarter_table():
    samples = np.arange(L // FOLD)
    bins = np.arange(FB) + F0
    phase = np.mod(samples[:, None] * bins[None, :], L) * (2.0 * math.pi / L)
    table = np.concatenate([np.cos(phase), -np.sin(phase)], axis=1)
    return table.astype(np.float32).astype(ml_dtypes.bfloat16)


def inverse_table():
    bins = np.arange(FB) + F0
    shifts = np.arange(LAGS) - LAGS // 2
    turn = np.mod(bins[:, None] * shifts[None, :], L).astype(np.float32) * np.float32(2.0 * math.pi / L)
    inverse = np.concatenate([np.cos(turn), -np.sin(turn)], axis=0) / math.sqrt(FB)
    return inverse.astype(ml_dtypes.bfloat16)


def dot(a, b):
    return jnp.dot(a, b, preferred_element_type=jnp.float32)


def iota(shape, axis):
    return lax.broadcasted_iota(jnp.int32, shape, axis)


def other(index, step):
    for bit in range(step.bit_length()):
        if (step >> bit) & 1:
            index = index + 2**bit - 2 ** (bit + 1) * ((index // 2**bit) % 2)
    return index


def build_toeplitz(taps_ref, wide_taps, toeplitz):
    wide_taps[...] = jnp.zeros_like(wide_taps)
    wide_taps[:, :TAPS] = taps_ref[...].astype(jnp.float32)
    moved = jnp.broadcast_to(wide_taps[...], (128, 256))
    row = iota((128, 256), 0)
    for bit in range(7):
        moved = jnp.where((row >> bit) & 1 == 1, pltpu.roll(moved, 2**bit, 1), moved)
    moved = moved.astype(jnp.bfloat16)
    here, before = moved[:, :128], moved[:, 128:]
    zero = jnp.zeros((128, 128), jnp.bfloat16)
    toeplitz[0:128, :] = jnp.concatenate([before, zero], axis=1)
    toeplitz[128:256, :] = jnp.concatenate([here, before], axis=1)
    toeplitz[256:384, :] = jnp.concatenate([zero, here], axis=1)


def whiten_rows(rows_ref, toeplitz, filt, size, normed, table, table_ready):
    count = rows_ref.shape[0]
    blocks = L // CHUNK
    group = 4
    zero = jnp.zeros((count, 128), jnp.bfloat16)
    for g in range(0, blocks, group):
        parts = [
            rows_ref[:, j * CHUNK - 128 : (j + 1) * CHUNK]
            if j
            else jnp.concatenate([zero, rows_ref[:, :CHUNK]], axis=1)
            for j in range(g, g + group)
        ]
        part = dot(jnp.concatenate(parts, axis=0), toeplitz[...])
        filt[g * count : (g + group) * count, :] = part
        size[g * count : (g + group) * count, :] = jnp.abs(part).astype(jnp.bfloat16)

    reach = jnp.abs(iota((512, CHUNK), 0) - 128 - iota((512, CHUNK), 1)) <= HALF
    band = reach.astype(jnp.float32).astype(jnp.bfloat16)
    for g in range(0, blocks, group):
        parts = []
        for j in range(g, g + group):
            low = size[(j - 1) * count : j * count, 128:] if j else zero
            high = size[(j + 1) * count : (j + 2) * count, :128] if j < blocks - 1 else zero
            parts.append(jnp.concatenate([low, size[j * count : (j + 1) * count, :], high], axis=1))
        total = dot(jnp.concatenate(parts, axis=0), band)
        for j in range(g, g + group):
            position = j * CHUNK + iota((1, CHUNK), 1)
            width = jnp.minimum(position, HALF) + jnp.minimum(L - 1 - position, HALF) + 1
            scale = 1.0 / width.astype(jnp.float32)
            fold, at = divmod(j * CHUNK, L // FOLD)
            normed[fold * count : (fold + 1) * count, at : at + CHUNK] = (
                filt[j * count : (j + 1) * count, :]
                / (total[(j - g) * count : (j - g + 1) * count] * scale + epsilon)
            ).astype(jnp.bfloat16)

    table_ready()
    quarters = dot(normed[...], table[...])
    k = iota((1, FB), 1) + F0
    real = imag = jnp.zeros((count, FB), jnp.float32)
    for fold in range(FOLD):
        turns = (k * fold) % 4
        cosine = jnp.where(turns == 0, 1.0, jnp.where(turns == 2, -1.0, 0.0))
        sine = jnp.where(turns == 1, 1.0, jnp.where(turns == 3, -1.0, 0.0))
        re = quarters[fold * count : (fold + 1) * count, :FB]
        im = quarters[fold * count : (fold + 1) * count, FB:]
        real = real + cosine * re + sine * im
        imag = imag + cosine * im - sine * re
    energy = real * real + imag * imag
    near = jnp.abs(iota((FB, FB), 0) - iota((FB, FB), 1)) <= SMOOTH
    near = near.astype(jnp.float32).astype(jnp.bfloat16)
    upper = energy.astype(jnp.bfloat16)
    left = energy - upper.astype(jnp.float32)
    middle = left.astype(jnp.bfloat16)
    lower = (left - middle.astype(jnp.float32)).astype(jnp.bfloat16)
    split = dot(jnp.concatenate([upper, middle, lower], axis=0), near)
    total = split[:count] + split[count : 2 * count] + split[2 * count :]
    k = iota((1, FB), 1)
    width = jnp.minimum(k, SMOOTH) + jnp.minimum(FB - 1 - k, SMOOTH) + 1
    smooth = total / width.astype(jnp.float32)
    level = jnp.sum(energy, axis=1, keepdims=True) * (1.0 / FB)
    factor = lax.rsqrt(smooth + water_level * level + epsilon)
    return real * factor, imag * factor


def spectra_kernel(sizes, taps_hbm, sources_hbm, label_hbm, file_ref, table_ref, turn_ref, chan_ref, src_ref, inverse_ref,
                   taps_ref, sources_ref, label_ref, rows, filt, size, normed, toeplitz, wide_taps, table, held, labels,
                   load_sems, send_sems, recv_sems, label_sems):
    zs, xs, cs = sizes
    z, x, c = lax.axis_index("chan"), lax.axis_index("win"), lax.axis_index("grp")
    share = rows.shape[0]
    count = share * cs
    own = pl.ds(pl.multiple_of(c * share, share), share)

    fetch = pltpu.make_async_copy(file_ref.at[own, :], rows, load_sems.at[0])
    fetch.start()
    small = []
    for source, target in ((taps_hbm, taps_ref), (label_hbm, label_ref), (sources_hbm, sources_ref)):
        copy = pltpu.make_async_copy(source, target, load_sems.at[3 + len(small)])
        copy.start()
        small.append(copy)
    load = pltpu.make_async_copy(table_ref, table, load_sems.at[1])
    load.start()
    turn = pltpu.make_async_copy(turn_ref, inverse_ref, load_sems.at[2])
    turn.start()

    barrier = pltpu.get_barrier_semaphore()
    swap = 1 if cs > 1 else 0
    partners = [{"chan": other(z, d), "grp": other(c, swap)} for d in range(1, zs)]
    partners += [{"win": other(x, e), "grp": other(c, swap)} for e in range(1, xs)]
    partners += [{"grp": other(c, f)} for f in range(1, cs)]
    for partner in partners:
        pl.semaphore_signal(barrier, inc=1, device_id=partner, device_id_type=pl.DeviceIdType.MESH)

    labels[0] = jnp.zeros(labels.shape[1:], jnp.int32)
    for copy in small:
        copy.wait()
    labels[0, :, :count] = label_ref[:, :count]
    build_toeplitz(taps_ref, wide_taps, toeplitz)
    fetch.wait()
    real, imag = whiten_rows(rows, toeplitz, filt, size, normed, table, load.wait)
    held[0, 0, own, :FB] = real.astype(jnp.bfloat16)
    held[0, 0, own, FB:] = imag.astype(jnp.bfloat16)

    pl.semaphore_wait(barrier, len(partners))

    copies = {}

    def send(d, e, f, source, target, mine):
        copy = pltpu.make_async_remote_copy(
            src_ref=held.at[source[1], source[0], mine],
            dst_ref=held.at[e, d, mine],
            send_sem=send_sems.at[d, e, f],
            recv_sem=recv_sems.at[d, e, f],
            device_id=target,
            device_id_type=pl.DeviceIdType.MESH,
        )
        copy.start()
        copies[d, e, f] = copy

    def along_win(d):
        for e in range(1, xs):
            send(d, e, 0, (d, 0), {"win": other(x, e), "grp": other(c, swap)}, brought(d, 0))

    def along_chan(d, e):
        send(d, e, 0, (0, e), {"chan": other(z, d), "grp": other(c, swap)}, brought(0, e))

    def along_grp(d, e):
        for f in range(1, cs):
            send(d, e, f, (d, e), {"grp": other(c, f)}, brought(d, e))

    def brought(d, e):
        core = other(c, swap * (((d > 0) + (e > 0)) % 2))
        return pl.ds(pl.multiple_of(core * share, share), share)

    across = zs - 1
    told = []
    for d in range(1, zs):
        copy = pltpu.make_async_remote_copy(
            src_ref=labels.at[0],
            dst_ref=labels.at[d],
            send_sem=label_sems.at[0, d],
            recv_sem=label_sems.at[1, d],
            device_id={"chan": other(z, d), "grp": other(c, swap)},
            device_id_type=pl.DeviceIdType.MESH,
        )
        copy.start()
        told.append(copy)
    along_win(0)
    for d in range(1, zs):
        along_chan(d, 0)
    along_grp(0, 0)

    groups, width = sources_ref.shape
    channels = chan_ref.shape[0]
    diagonal = iota((width, width), 0) == iota((width, width), 1)
    wanted = [
        jnp.sum(jnp.where(diagonal, sources_ref[g : g + 1, :], 0), axis=1, keepdims=True)
        for g in range(groups)
    ]
    wanted.append(z * CH_DEV + x * channels + iota((channels, 1), 0))
    wanted = jnp.concatenate(wanted, axis=0)

    for e in range(1, xs):
        copies[0, e, 0].wait_recv()
        if across:
            along_chan(across, e)
        along_grp(0, e)
    for d in range(1, zs):
        copies[d, 0, 0].wait_recv()
        if d != across:
            along_win(d)
        along_grp(d, 0)

    for copy in told:
        copy.wait()
    span = max(1, 2 * FB // count)
    picks = []
    for d in range(0, zs, span):
        names = jnp.concatenate([labels[d + i, :, :count] for i in range(min(span, zs - d))], axis=1)
        picks.append((wanted == names).astype(jnp.float32).astype(jnp.bfloat16))

    def select(e):
        total = None
        for d, pick in zip(range(0, zs, span), picks):
            block = held[e, d : d + span]
            part = dot(pick, block.reshape(block.shape[0] * count, 2 * FB))
            total = part if total is None else total + part
        at = e * 2 * FB
        src_ref[:, at : at + 2 * FB] = total[: groups * width].astype(jnp.bfloat16)
        chan_ref[:, at : at + 2 * FB] = total[groups * width :]

    for d in range(zs):
        for f in range(1, cs):
            copies[d, 0, f].wait_recv()
    select(0)
    for e in range(1, xs):
        for d in range(1, zs):
            copies[d, e, 0].wait_recv()
            along_grp(d, e)
    for e in range(1, xs):
        for d in range(zs):
            for f in range(1, cs):
                copies[d, e, f].wait_recv()
        select(e)
    for copy in copies.values():
        copy.wait_send()
    turn.wait()


def correlate_kernel(wins, steps, inverse_ref, src_ref, chan_ref, out_ref, made, sems):
    inverse = inverse_ref[...]
    copies = []
    begin = 0
    for step in steps:
        for c in range(begin, begin + step):
            real = imag = None
            for w in range(wins):
                at = w * 2 * FB
                p, q = src_ref[:, at : at + FB], src_ref[:, at + FB : at + 2 * FB]
                row = chan_ref[c : c + 1, at : at + 2 * FB].astype(jnp.bfloat16)
                a, b = row[:, :FB], row[:, FB:]
                re, im = a * p + b * q, b * p - a * q
                real = re if real is None else real + re
                imag = im if imag is None else imag + im
            made[c] = dot(jnp.concatenate([real, imag], axis=1), inverse)
        part = pl.ds(begin, step)
        copy = pltpu.make_async_copy(made.at[part], out_ref.at[part], sems.at[len(copies)])
        copy.start()
        copies.append(copy)
        begin += step
    for copy in copies:
        copy.wait()


def local(file_rows, channel_list, filter_taps, source_channels):
    chan_count = lax.axis_size("chan")
    wins = lax.axis_size("win")
    cores = lax.axis_size("grp")
    count = chan_count * (CH_DEV // 4)
    share = count // cores
    channels = CH_DEV // wins
    groups, width = source_channels.shape
    sources = groups * width
    assert file_rows.shape[1] == L

    vmem = pl.BlockSpec(memory_space=pltpu.VMEM)
    hbm = pl.BlockSpec(memory_space=pltpu.HBM)
    given = (
        filter_taps.reshape(1, TAPS),
        source_channels,
        channel_list.reshape(1, -1),
        file_rows,
        jnp.asarray(quarter_table()),
        jnp.asarray(inverse_table()),
    )
    chan_spec, src_spec, inverse = pl.pallas_call(
        functools.partial(spectra_kernel, (chan_count, wins, cores)),
        in_specs=[hbm] * 6,
        out_specs=[vmem] * 3,
        out_shape=[
            pltpu.VMEM((channels, wins * 2 * FB), jnp.float32),
            pltpu.VMEM((sources, wins * 2 * FB), jnp.bfloat16),
            pltpu.VMEM((2 * FB, LAGS), jnp.bfloat16),
        ],
        scratch_shapes=[
            pltpu.VMEM((1, TAPS), jnp.bfloat16),
            pltpu.VMEM((groups, width), jnp.int32),
            pltpu.VMEM((1, channel_list.shape[0]), jnp.int32),
            pltpu.VMEM((share, L), jnp.bfloat16),
            pltpu.VMEM((L // CHUNK * share, CHUNK), jnp.float32),
            pltpu.VMEM((L // CHUNK * share, CHUNK), jnp.bfloat16),
            pltpu.VMEM((FOLD * share, L // FOLD), jnp.bfloat16),
            pltpu.VMEM((384, 256), jnp.bfloat16),
            pltpu.VMEM((1, 256), jnp.float32),
            pltpu.VMEM((L // FOLD, 2 * FB), jnp.bfloat16),
            pltpu.VMEM((wins, chan_count, count, 2 * FB), jnp.bfloat16),
            pltpu.VMEM((chan_count, 1, -(-count // 128) * 128), jnp.int32),
            pltpu.SemaphoreType.DMA((6,)),
            pltpu.SemaphoreType.DMA((chan_count, wins, cores)),
            pltpu.SemaphoreType.DMA((chan_count, wins, cores)),
            pltpu.SemaphoreType.DMA((2, chan_count)),
        ],
        compiler_params=pltpu.CompilerParams(
            collective_id=0, has_side_effects=True, vmem_limit_bytes=SPECTRA_VMEM
        ),
        name="spectra",
    )(*(pltpu.with_memory_space_constraint(array, pltpu.HBM) for array in given))

    step = min(8, channels // 2)
    edge = step // 2
    steps = (edge,) + (step,) * (channels // step - 1) + (edge,)
    return pl.pallas_call(
        functools.partial(correlate_kernel, wins, steps),
        in_specs=[vmem, vmem, vmem],
        out_specs=pl.BlockSpec(memory_space=pl.ANY),
        out_shape=jax.ShapeDtypeStruct((channels, sources, LAGS), jnp.float32),
        scratch_shapes=[
            pltpu.VMEM((channels, sources, LAGS), jnp.float32),
            pltpu.SemaphoreType.DMA((len(steps),)),
        ],
        compiler_params=pltpu.CompilerParams(vmem_limit_bytes=CORRELATE_VMEM),
        name="correlate",
    )(inverse, src_spec, chan_spec)


def solution(mesh):
    placed = (P(("fibre", "chan"), "win"), P(("fibre", "chan")), P(), P(("fibre", "grp"), None))
    return jax.shard_map(
        local,
        mesh=mesh,
        in_specs=placed,
        out_specs=P(("fibre", "chan", "win"), "grp", None),
        check_vma=False,
    )
```

```python
import functools
import math

import jax
import jax.numpy as jnp
import ml_dtypes
import numpy as np
from jax import lax
from jax.experimental import pallas as pl
from jax.experimental.pallas import tpu as pltpu
from jax.sharding import PartitionSpec as P

L = 4096
FB = 256
F0 = 8
LAGS = 256
TAPS = 64
HALF = 64
SMOOTH = 8
CH_DEV = 128
FOLD = 4
CHUNK = 256
SPECTRA_VMEM = 52 * 1024 * 1024
CORRELATE_VMEM = 40 * 1024 * 1024

epsilon = 1e-06
water_level = 0.1


def quarter_table():
    samples = np.arange(L // FOLD)
    bins = np.arange(FB) + F0
    phase = np.mod(samples[:, None] * bins[None, :], L) * (2.0 * math.pi / L)
    table = np.concatenate([np.cos(phase), -np.sin(phase)], axis=1)
    return table.astype(np.float32).astype(ml_dtypes.bfloat16)


def inverse_table():
    bins = np.arange(FB) + F0
    shifts = np.arange(LAGS) - LAGS // 2
    turn = np.mod(bins[:, None] * shifts[None, :], L).astype(np.float32) * np.float32(2.0 * math.pi / L)
    inverse = np.concatenate([np.cos(turn), -np.sin(turn)], axis=0) / math.sqrt(FB)
    return inverse.astype(ml_dtypes.bfloat16)


def dot(a, b):
    return jnp.dot(a, b, preferred_element_type=jnp.float32)


def iota(shape, axis):
    return lax.broadcasted_iota(jnp.int32, shape, axis)


def other(index, step):
    for bit in range(step.bit_length()):
        if (step >> bit) & 1:
            index = index + 2**bit - 2 ** (bit + 1) * ((index // 2**bit) % 2)
    return index


def build_toeplitz(taps_ref, wide_taps, toeplitz):
    wide_taps[...] = jnp.zeros_like(wide_taps)
    wide_taps[:, :TAPS] = taps_ref[...].astype(jnp.float32)
    moved = jnp.broadcast_to(wide_taps[...], (128, 256))
    row = iota((128, 256), 0)
    for bit in range(7):
        moved = jnp.where((row >> bit) & 1 == 1, pltpu.roll(moved, 2**bit, 1), moved)
    moved = moved.astype(jnp.bfloat16)
    here, before = moved[:, :128], moved[:, 128:]
    zero = jnp.zeros((128, 128), jnp.bfloat16)
    toeplitz[0:128, :] = jnp.concatenate([before, zero], axis=1)
    toeplitz[128:256, :] = jnp.concatenate([here, before], axis=1)
    toeplitz[256:384, :] = jnp.concatenate([zero, here], axis=1)


def whiten_rows(rows_ref, toeplitz, filt, size, normed, table, table_ready):
    count = rows_ref.shape[0]
    blocks = L // CHUNK
    group = 4
    zero = jnp.zeros((count, 128), jnp.bfloat16)
    for g in range(0, blocks, group):
        parts = [
            rows_ref[:, j * CHUNK - 128 : (j + 1) * CHUNK]
            if j
            else jnp.concatenate([zero, rows_ref[:, :CHUNK]], axis=1)
            for j in range(g, g + group)
        ]
        part = dot(jnp.concatenate(parts, axis=0), toeplitz[...])
        filt[g * count : (g + group) * count, :] = part
        size[g * count : (g + group) * count, :] = jnp.abs(part).astype(jnp.bfloat16)

    reach = jnp.abs(iota((512, CHUNK), 0) - 128 - iota((512, CHUNK), 1)) <= HALF
    band = reach.astype(jnp.float32).astype(jnp.bfloat16)
    for g in range(0, blocks, group):
        parts = []
        for j in range(g, g + group):
            low = size[(j - 1) * count : j * count, 128:] if j else zero
            high = size[(j + 1) * count : (j + 2) * count, :128] if j < blocks - 1 else zero
            parts.append(jnp.concatenate([low, size[j * count : (j + 1) * count, :], high], axis=1))
        total = dot(jnp.concatenate(parts, axis=0), band)
        for j in range(g, g + group):
            position = j * CHUNK + iota((1, CHUNK), 1)
            width = jnp.minimum(position, HALF) + jnp.minimum(L - 1 - position, HALF) + 1
            scale = 1.0 / width.astype(jnp.float32)
            fold, at = divmod(j * CHUNK, L // FOLD)
            normed[fold * count : (fold + 1) * count, at : at + CHUNK] = (
                filt[j * count : (j + 1) * count, :]
                / (total[(j - g) * count : (j - g + 1) * count] * scale + epsilon)
            ).astype(jnp.bfloat16)

    table_ready()
    quarters = dot(normed[...], table[...])
    k = iota((1, FB), 1) + F0
    real = imag = jnp.zeros((count, FB), jnp.float32)
    for fold in range(FOLD):
        turns = (k * fold) % 4
        cosine = jnp.where(turns == 0, 1.0, jnp.where(turns == 2, -1.0, 0.0))
        sine = jnp.where(turns == 1, 1.0, jnp.where(turns == 3, -1.0, 0.0))
        re = quarters[fold * count : (fold + 1) * count, :FB]
        im = quarters[fold * count : (fold + 1) * count, FB:]
        real = real + cosine * re + sine * im
        imag = imag + cosine * im - sine * re
    energy = real * real + imag * imag
    near = jnp.abs(iota((FB, FB), 0) - iota((FB, FB), 1)) <= SMOOTH
    near = near.astype(jnp.float32).astype(jnp.bfloat16)
    upper = energy.astype(jnp.bfloat16)
    left = energy - upper.astype(jnp.float32)
    middle = left.astype(jnp.bfloat16)
    lower = (left - middle.astype(jnp.float32)).astype(jnp.bfloat16)
    split = dot(jnp.concatenate([upper, middle, lower], axis=0), near)
    total = split[:count] + split[count : 2 * count] + split[2 * count :]
    k = iota((1, FB), 1)
    width = jnp.minimum(k, SMOOTH) + jnp.minimum(FB - 1 - k, SMOOTH) + 1
    smooth = total / width.astype(jnp.float32)
    level = jnp.sum(energy, axis=1, keepdims=True) * (1.0 / FB)
    factor = lax.rsqrt(smooth + water_level * level + epsilon)
    return real * factor, imag * factor


def spectra_kernel(sizes, taps_hbm, sources_hbm, label_hbm, file_ref, table_ref, turn_ref, chan_ref, src_ref, inverse_ref,
                   taps_ref, sources_ref, label_ref, rows, filt, size, normed, toeplitz, wide_taps, table, held, labels,
                   load_sems, send_sems, recv_sems, label_sems):
    zs, xs, cs = sizes
    z, x, c = lax.axis_index("chan"), lax.axis_index("win"), lax.axis_index("grp")
    share = rows.shape[0]
    count = share * cs
    own = pl.ds(pl.multiple_of(c * share, share), share)

    small = []
    for source, target in ((taps_hbm, taps_ref), (label_hbm, label_ref), (sources_hbm, sources_ref)):
        copy = pltpu.make_async_copy(source, target, load_sems.at[3 + len(small)])
        copy.start()
        small.append(copy)
    fetch = pltpu.make_async_copy(file_ref.at[own, :], rows, load_sems.at[0])
    fetch.start()
    load = pltpu.make_async_copy(table_ref, table, load_sems.at[1])
    load.start()
    turn = pltpu.make_async_copy(turn_ref, inverse_ref, load_sems.at[2])
    turn.start()

    barrier = pltpu.get_barrier_semaphore()
    swap = 1 if cs > 1 else 0
    partners = [{"chan": other(z, d), "grp": other(c, swap)} for d in range(1, zs)]
    partners += [{"win": other(x, e), "grp": other(c, swap)} for e in range(1, xs)]
    partners += [{"grp": other(c, f)} for f in range(1, cs)]
    for partner in partners:
        pl.semaphore_signal(barrier, inc=1, device_id=partner, device_id_type=pl.DeviceIdType.MESH)

    labels[0] = jnp.zeros(labels.shape[1:], jnp.int32)
    for copy in small:
        copy.wait()
    labels[0, :, :count] = label_ref[:, :count]
    build_toeplitz(taps_ref, wide_taps, toeplitz)
    fetch.wait()
    real, imag = whiten_rows(rows, toeplitz, filt, size, normed, table, load.wait)
    held[0, 0, own, :FB] = real.astype(jnp.bfloat16)
    held[0, 0, own, FB:] = imag.astype(jnp.bfloat16)

    pl.semaphore_wait(barrier, len(partners))

    copies = {}

    def send(d, e, f, source, target, mine):
        copy = pltpu.make_async_remote_copy(
            src_ref=held.at[source[1], source[0], mine],
            dst_ref=held.at[e, d, mine],
            send_sem=send_sems.at[d, e, f],
            recv_sem=recv_sems.at[d, e, f],
            device_id=target,
            device_id_type=pl.DeviceIdType.MESH,
        )
        copy.start()
        copies[d, e, f] = copy

    def along_win(d):
        for e in range(1, xs):
            send(d, e, 0, (d, 0), {"win": other(x, e), "grp": other(c, swap)}, brought(d, 0))

    def along_chan(d, e):
        send(d, e, 0, (0, e), {"chan": other(z, d), "grp": other(c, swap)}, brought(0, e))

    def along_grp(d, e):
        for f in range(1, cs):
            send(d, e, f, (d, e), {"grp": other(c, f)}, brought(d, e))

    def brought(d, e):
        core = other(c, swap * (((d > 0) + (e > 0)) % 2))
        return pl.ds(pl.multiple_of(core * share, share), share)

    across = zs - 1
    told = []
    for d in range(1, zs):
        copy = pltpu.make_async_remote_copy(
            src_ref=labels.at[0],
            dst_ref=labels.at[d],
            send_sem=label_sems.at[0, d],
            recv_sem=label_sems.at[1, d],
            device_id={"chan": other(z, d), "grp": other(c, swap)},
            device_id_type=pl.DeviceIdType.MESH,
        )
        copy.start()
        told.append(copy)
    along_win(0)
    for d in range(1, zs):
        along_chan(d, 0)
    along_grp(0, 0)

    groups, width = sources_ref.shape
    channels = chan_ref.shape[0]
    diagonal = iota((width, width), 0) == iota((width, width), 1)
    wanted = [
        jnp.sum(jnp.where(diagonal, sources_ref[g : g + 1, :], 0), axis=1, keepdims=True)
        for g in range(groups)
    ]
    wanted.append(z * CH_DEV + x * channels + iota((channels, 1), 0))
    wanted = jnp.concatenate(wanted, axis=0)

    for e in range(1, xs):
        copies[0, e, 0].wait_recv()
        if across:
            along_chan(across, e)
        along_grp(0, e)
    for d in range(1, zs):
        copies[d, 0, 0].wait_recv()
        if d != across:
            along_win(d)
        along_grp(d, 0)

    for copy in told:
        copy.wait()
    span = max(1, 2 * FB // count)
    picks = []
    for d in range(0, zs, span):
        names = jnp.concatenate([labels[d + i, :, :count] for i in range(min(span, zs - d))], axis=1)
        picks.append((wanted == names).astype(jnp.float32).astype(jnp.bfloat16))

    def select(e):
        total = None
        for d, pick in zip(range(0, zs, span), picks):
            block = held[e, d : d + span]
            part = dot(pick, block.reshape(block.shape[0] * count, 2 * FB))
            total = part if total is None else total + part
        at = e * 2 * FB
        src_ref[:, at : at + 2 * FB] = total[: groups * width].astype(jnp.bfloat16)
        chan_ref[:, at : at + 2 * FB] = total[groups * width :]

    for d in range(zs):
        for f in range(1, cs):
            copies[d, 0, f].wait_recv()
    select(0)
    for e in range(1, xs):
        for d in range(1, zs):
            copies[d, e, 0].wait_recv()
            along_grp(d, e)
    for e in range(1, xs):
        for d in range(zs):
            for f in range(1, cs):
                copies[d, e, f].wait_recv()
        select(e)
    for copy in copies.values():
        copy.wait_send()
    turn.wait()


def correlate_kernel(wins, steps, inverse_ref, src_ref, chan_ref, out_ref, made, sems):
    inverse = inverse_ref[...]
    copies = []
    begin = 0
    for step in steps:
        pair = 2 if step % 2 == 0 else 1
        for first in range(begin, begin + step, pair):
            cross = []
            for c in range(first, first + pair):
                real = imag = None
                for w in range(wins):
                    at = w * 2 * FB
                    p, q = src_ref[:, at : at + FB], src_ref[:, at + FB : at + 2 * FB]
                    row = chan_ref[c : c + 1, at : at + 2 * FB].astype(jnp.bfloat16)
                    a, b = row[:, :FB], row[:, FB:]
                    re, im = a * p + b * q, b * p - a * q
                    real = re if real is None else real + re
                    imag = im if imag is None else imag + im
                cross.append(jnp.concatenate([real, imag], axis=1))
            result = dot(jnp.concatenate(cross, axis=0), inverse)
            made[first : first + pair] = result.reshape(pair, *made.shape[1:])
        part = pl.ds(begin, step)
        copy = pltpu.make_async_copy(made.at[part], out_ref.at[part], sems.at[len(copies)])
        copy.start()
        copies.append(copy)
        begin += step
    for copy in copies:
        copy.wait()


def local(file_rows, channel_list, filter_taps, source_channels):
    chan_count = lax.axis_size("chan")
    wins = lax.axis_size("win")
    cores = lax.axis_size("grp")
    count = chan_count * (CH_DEV // 4)
    share = count // cores
    channels = CH_DEV // wins
    groups, width = source_channels.shape
    sources = groups * width
    assert file_rows.shape[1] == L

    vmem = pl.BlockSpec(memory_space=pltpu.VMEM)
    hbm = pl.BlockSpec(memory_space=pltpu.HBM)
    given = (
        filter_taps.reshape(1, TAPS),
        source_channels,
        channel_list.reshape(1, -1),
        file_rows,
        jnp.asarray(quarter_table()),
        jnp.asarray(inverse_table()),
    )
    chan_spec, src_spec, inverse = pl.pallas_call(
        functools.partial(spectra_kernel, (chan_count, wins, cores)),
        in_specs=[hbm] * 6,
        out_specs=[vmem] * 3,
        out_shape=[
            pltpu.VMEM((channels, wins * 2 * FB), jnp.float32),
            pltpu.VMEM((sources, wins * 2 * FB), jnp.bfloat16),
            pltpu.VMEM((2 * FB, LAGS), jnp.bfloat16),
        ],
        scratch_shapes=[
            pltpu.VMEM((1, TAPS), jnp.bfloat16),
            pltpu.VMEM((groups, width), jnp.int32),
            pltpu.VMEM((1, channel_list.shape[0]), jnp.int32),
            pltpu.VMEM((share, L), jnp.bfloat16),
            pltpu.VMEM((L // CHUNK * share, CHUNK), jnp.float32),
            pltpu.VMEM((L // CHUNK * share, CHUNK), jnp.bfloat16),
            pltpu.VMEM((FOLD * share, L // FOLD), jnp.bfloat16),
            pltpu.VMEM((384, 256), jnp.bfloat16),
            pltpu.VMEM((1, 256), jnp.float32),
            pltpu.VMEM((L // FOLD, 2 * FB), jnp.bfloat16),
            pltpu.VMEM((wins, chan_count, count, 2 * FB), jnp.bfloat16),
            pltpu.VMEM((chan_count, 1, -(-count // 128) * 128), jnp.int32),
            pltpu.SemaphoreType.DMA((6,)),
            pltpu.SemaphoreType.DMA((chan_count, wins, cores)),
            pltpu.SemaphoreType.DMA((chan_count, wins, cores)),
            pltpu.SemaphoreType.DMA((2, chan_count)),
        ],
        compiler_params=pltpu.CompilerParams(
            collective_id=0, has_side_effects=True, vmem_limit_bytes=SPECTRA_VMEM
        ),
        name="spectra",
    )(*(pltpu.with_memory_space_constraint(array, pltpu.HBM) for array in given))

    step = min(4, channels)
    steps = (step,) * (channels // step)
    return pl.pallas_call(
        functools.partial(correlate_kernel, wins, steps),
        in_specs=[vmem, vmem, vmem],
        out_specs=pl.BlockSpec(memory_space=pl.ANY),
        out_shape=jax.ShapeDtypeStruct((channels, sources, LAGS), jnp.float32),
        scratch_shapes=[
            pltpu.VMEM((channels, sources, LAGS), jnp.float32),
            pltpu.SemaphoreType.DMA((len(steps),)),
        ],
        compiler_params=pltpu.CompilerParams(vmem_limit_bytes=CORRELATE_VMEM),
        name="correlate",
    )(inverse, src_spec, chan_spec)


def solution(mesh):
    placed = (P(("fibre", "chan"), "win"), P(("fibre", "chan")), P(), P(("fibre", "grp"), None))
    return jax.shard_map(
        local,
        mesh=mesh,
        in_specs=placed,
        out_specs=P(("fibre", "chan", "win"), "grp", None),
        check_vma=False,
    )
```

```python
import functools
import math

import jax
import jax.numpy as jnp
import ml_dtypes
import numpy as np
from jax import lax
from jax.experimental import pallas as pl
from jax.experimental.pallas import tpu as pltpu
from jax.sharding import PartitionSpec as P

L = 4096
FB = 256
F0 = 8
LAGS = 256
TAPS = 64
HALF = 64
SMOOTH = 8
CH_DEV = 128
FOLD = 4
CHUNK = 256
SPECTRA_VMEM = 52 * 1024 * 1024
CORRELATE_VMEM = 40 * 1024 * 1024

epsilon = 1e-06
water_level = 0.1


def quarter_table():
    samples = np.arange(L // FOLD)
    bins = np.arange(FB) + F0
    phase = np.mod(samples[:, None] * bins[None, :], L) * (2.0 * math.pi / L)
    table = np.concatenate([np.cos(phase), -np.sin(phase)], axis=1)
    return table.astype(np.float32).astype(ml_dtypes.bfloat16)


def inverse_table():
    bins = np.arange(FB) + F0
    shifts = np.arange(LAGS) - LAGS // 2
    turn = np.mod(bins[:, None] * shifts[None, :], L).astype(np.float32) * np.float32(2.0 * math.pi / L)
    inverse = np.concatenate([np.cos(turn), -np.sin(turn)], axis=0) / math.sqrt(FB)
    return inverse.astype(ml_dtypes.bfloat16)


def dot(a, b):
    return jnp.dot(a, b, preferred_element_type=jnp.float32)


def iota(shape, axis):
    return lax.broadcasted_iota(jnp.int32, shape, axis)


def other(index, step):
    for bit in range(step.bit_length()):
        if (step >> bit) & 1:
            index = index + 2**bit - 2 ** (bit + 1) * ((index // 2**bit) % 2)
    return index


def build_toeplitz(taps_ref, wide_taps, toeplitz):
    wide_taps[...] = jnp.zeros_like(wide_taps)
    wide_taps[:, :TAPS] = taps_ref[...].astype(jnp.float32)
    moved = jnp.broadcast_to(wide_taps[...], (128, 256))
    row = iota((128, 256), 0)
    for bit in range(7):
        moved = jnp.where((row >> bit) & 1 == 1, pltpu.roll(moved, 2**bit, 1), moved)
    moved = moved.astype(jnp.bfloat16)
    here, before = moved[:, :128], moved[:, 128:]
    zero = jnp.zeros((128, 128), jnp.bfloat16)
    toeplitz[0:128, :] = jnp.concatenate([before, zero], axis=1)
    toeplitz[128:256, :] = jnp.concatenate([here, before], axis=1)
    toeplitz[256:384, :] = jnp.concatenate([zero, here], axis=1)


def whiten_rows(rows_ref, toeplitz, filt, size, normed, table, table_ready):
    count = rows_ref.shape[0]
    blocks = L // CHUNK
    group = 4
    zero = jnp.zeros((count, 128), jnp.bfloat16)
    for g in range(0, blocks, group):
        parts = [
            rows_ref[:, j * CHUNK - 128 : (j + 1) * CHUNK]
            if j
            else jnp.concatenate([zero, rows_ref[:, :CHUNK]], axis=1)
            for j in range(g, g + group)
        ]
        part = dot(jnp.concatenate(parts, axis=0), toeplitz[...])
        filt[g * count : (g + group) * count, :] = part
        size[g * count : (g + group) * count, :] = jnp.abs(part).astype(jnp.bfloat16)

    reach = jnp.abs(iota((512, CHUNK), 0) - 128 - iota((512, CHUNK), 1)) <= HALF
    band = reach.astype(jnp.float32).astype(jnp.bfloat16)
    for g in range(0, blocks, group):
        parts = []
        for j in range(g, g + group):
            low = size[(j - 1) * count : j * count, 128:] if j else zero
            high = size[(j + 1) * count : (j + 2) * count, :128] if j < blocks - 1 else zero
            parts.append(jnp.concatenate([low, size[j * count : (j + 1) * count, :], high], axis=1))
        total = dot(jnp.concatenate(parts, axis=0), band)
        for j in range(g, g + group):
            position = j * CHUNK + iota((1, CHUNK), 1)
            width = jnp.minimum(position, HALF) + jnp.minimum(L - 1 - position, HALF) + 1
            scale = 1.0 / width.astype(jnp.float32)
            fold, at = divmod(j * CHUNK, L // FOLD)
            normed[fold * count : (fold + 1) * count, at : at + CHUNK] = (
                filt[j * count : (j + 1) * count, :]
                / (total[(j - g) * count : (j - g + 1) * count] * scale + epsilon)
            ).astype(jnp.bfloat16)

    table_ready()
    quarters = dot(normed[...], table[...])
    k = iota((1, FB), 1) + F0
    real = imag = jnp.zeros((count, FB), jnp.float32)
    for fold in range(FOLD):
        turns = (k * fold) % 4
        cosine = jnp.where(turns == 0, 1.0, jnp.where(turns == 2, -1.0, 0.0))
        sine = jnp.where(turns == 1, 1.0, jnp.where(turns == 3, -1.0, 0.0))
        re = quarters[fold * count : (fold + 1) * count, :FB]
        im = quarters[fold * count : (fold + 1) * count, FB:]
        real = real + cosine * re + sine * im
        imag = imag + cosine * im - sine * re
    energy = real * real + imag * imag
    near = jnp.abs(iota((FB, FB), 0) - iota((FB, FB), 1)) <= SMOOTH
    near = near.astype(jnp.float32).astype(jnp.bfloat16)
    upper = energy.astype(jnp.bfloat16)
    left = energy - upper.astype(jnp.float32)
    middle = left.astype(jnp.bfloat16)
    lower = (left - middle.astype(jnp.float32)).astype(jnp.bfloat16)
    split = dot(jnp.concatenate([upper, middle, lower], axis=0), near)
    total = split[:count] + split[count : 2 * count] + split[2 * count :]
    k = iota((1, FB), 1)
    width = jnp.minimum(k, SMOOTH) + jnp.minimum(FB - 1 - k, SMOOTH) + 1
    smooth = total / width.astype(jnp.float32)
    level = jnp.sum(energy, axis=1, keepdims=True) * (1.0 / FB)
    factor = lax.rsqrt(smooth + water_level * level + epsilon)
    return real * factor, imag * factor


def spectra_kernel(sizes, taps_hbm, sources_hbm, label_hbm, file_ref, table_ref, turn_ref, chan_ref, src_ref, inverse_ref,
                   taps_ref, sources_ref, label_ref, rows, filt, size, normed, toeplitz, wide_taps, table, held, labels,
                   load_sems, send_sems, recv_sems, label_sems):
    zs, xs, cs = sizes
    z, x, c = lax.axis_index("chan"), lax.axis_index("win"), lax.axis_index("grp")
    share = rows.shape[0]
    count = share * cs
    own = pl.ds(pl.multiple_of(c * share, share), share)

    small = []
    for source, target in ((taps_hbm, taps_ref), (label_hbm, label_ref), (sources_hbm, sources_ref)):
        copy = pltpu.make_async_copy(source, target, load_sems.at[3 + len(small)])
        copy.start()
        small.append(copy)
    fetch = pltpu.make_async_copy(file_ref.at[own, :], rows, load_sems.at[0])
    fetch.start()
    load = pltpu.make_async_copy(table_ref, table, load_sems.at[1])
    load.start()
    turn = pltpu.make_async_copy(turn_ref, inverse_ref, load_sems.at[2])
    turn.start()

    barrier = pltpu.get_barrier_semaphore()
    swap = 1 if cs > 1 else 0
    partners = [{"chan": other(z, d), "grp": other(c, swap)} for d in range(1, zs)]
    partners += [{"win": other(x, e), "grp": other(c, swap)} for e in range(1, xs)]
    partners += [{"grp": other(c, f)} for f in range(1, cs)]
    for partner in partners:
        pl.semaphore_signal(barrier, inc=1, device_id=partner, device_id_type=pl.DeviceIdType.MESH)

    labels[0] = jnp.zeros(labels.shape[1:], jnp.int32)
    for copy in small:
        copy.wait()
    labels[0, :, :count] = label_ref[:, :count]
    build_toeplitz(taps_ref, wide_taps, toeplitz)
    fetch.wait()
    real, imag = whiten_rows(rows, toeplitz, filt, size, normed, table, load.wait)
    held[0, 0, own, :FB] = real.astype(jnp.bfloat16)
    held[0, 0, own, FB:] = imag.astype(jnp.bfloat16)

    pl.semaphore_wait(barrier, len(partners))

    copies = {}

    def send(d, e, f, source, target, mine):
        copy = pltpu.make_async_remote_copy(
            src_ref=held.at[source[1], source[0], mine],
            dst_ref=held.at[e, d, mine],
            send_sem=send_sems.at[d, e, f],
            recv_sem=recv_sems.at[d, e, f],
            device_id=target,
            device_id_type=pl.DeviceIdType.MESH,
        )
        copy.start()
        copies[d, e, f] = copy

    def along_win(d):
        for e in range(1, xs):
            send(d, e, 0, (d, 0), {"win": other(x, e), "grp": other(c, swap)}, brought(d, 0))

    def along_chan(d, e):
        send(d, e, 0, (0, e), {"chan": other(z, d), "grp": other(c, swap)}, brought(0, e))

    def along_grp(d, e):
        for f in range(1, cs):
            send(d, e, f, (d, e), {"grp": other(c, f)}, brought(d, e))

    def brought(d, e):
        core = other(c, swap * (((d > 0) + (e > 0)) % 2))
        return pl.ds(pl.multiple_of(core * share, share), share)

    across = zs - 1
    told = []
    for d in range(1, zs):
        copy = pltpu.make_async_remote_copy(
            src_ref=labels.at[0],
            dst_ref=labels.at[d],
            send_sem=label_sems.at[0, d],
            recv_sem=label_sems.at[1, d],
            device_id={"chan": other(z, d), "grp": other(c, swap)},
            device_id_type=pl.DeviceIdType.MESH,
        )
        copy.start()
        told.append(copy)
    along_win(0)
    for d in range(1, zs):
        along_chan(d, 0)
    along_grp(0, 0)

    groups, width = sources_ref.shape
    channels = chan_ref.shape[0]
    diagonal = iota((width, width), 0) == iota((width, width), 1)
    wanted = [
        jnp.sum(jnp.where(diagonal, sources_ref[g : g + 1, :], 0), axis=1, keepdims=True)
        for g in range(groups)
    ]
    wanted.append(z * CH_DEV + x * channels + iota((channels, 1), 0))
    wanted = jnp.concatenate(wanted, axis=0)

    for d in range(1, across):
        copies[d, 0, 0].wait_recv()
        along_win(d)
        along_grp(d, 0)
    for e in range(1, xs):
        copies[0, e, 0].wait_recv()
        if across:
            along_chan(across, e)
        along_grp(0, e)
    if across:
        copies[across, 0, 0].wait_recv()
        along_grp(across, 0)

    for copy in told:
        copy.wait()
    span = max(1, 2 * FB // count)
    picks = []
    for d in range(0, zs, span):
        names = jnp.concatenate([labels[d + i, :, :count] for i in range(min(span, zs - d))], axis=1)
        picks.append((wanted == names).astype(jnp.float32).astype(jnp.bfloat16))

    def select(e):
        total = None
        for d, pick in zip(range(0, zs, span), picks):
            block = held[e, d : d + span]
            part = dot(pick, block.reshape(block.shape[0] * count, 2 * FB))
            total = part if total is None else total + part
        at = e * 2 * FB
        src_ref[:, at : at + 2 * FB] = total[: groups * width].astype(jnp.bfloat16)
        chan_ref[:, at : at + 2 * FB] = total[groups * width :]

    for e in range(1, xs):
        for d in range(1, zs):
            copies[d, e, 0].wait_recv()
            along_grp(d, e)
    for d in range(zs):
        for f in range(1, cs):
            copies[d, 0, f].wait_recv()
    select(0)
    for e in range(1, xs):
        for d in range(zs):
            for f in range(1, cs):
                copies[d, e, f].wait_recv()
        select(e)
    for copy in copies.values():
        copy.wait_send()
    turn.wait()


def correlate_kernel(wins, steps, inverse_ref, src_ref, chan_ref, out_ref, made, sems):
    inverse = inverse_ref[...]
    copies = []
    begin = 0
    for step in steps:
        pair = 2 if step % 2 == 0 else 1
        for first in range(begin, begin + step, pair):
            cross = []
            for c in range(first, first + pair):
                real = imag = None
                for w in range(wins):
                    at = w * 2 * FB
                    p, q = src_ref[:, at : at + FB], src_ref[:, at + FB : at + 2 * FB]
                    row = chan_ref[c : c + 1, at : at + 2 * FB].astype(jnp.bfloat16)
                    a, b = row[:, :FB], row[:, FB:]
                    re, im = a * p + b * q, b * p - a * q
                    real = re if real is None else real + re
                    imag = im if imag is None else imag + im
                cross.append(jnp.concatenate([real, imag], axis=1))
            result = dot(jnp.concatenate(cross, axis=0), inverse)
            made[first : first + pair] = result.reshape(pair, *made.shape[1:])
        part = pl.ds(begin, step)
        copy = pltpu.make_async_copy(made.at[part], out_ref.at[part], sems.at[len(copies)])
        copy.start()
        copies.append(copy)
        begin += step
    for copy in copies:
        copy.wait()


def local(file_rows, channel_list, filter_taps, source_channels):
    chan_count = lax.axis_size("chan")
    wins = lax.axis_size("win")
    cores = lax.axis_size("grp")
    count = chan_count * (CH_DEV // 4)
    share = count // cores
    channels = CH_DEV // wins
    groups, width = source_channels.shape
    sources = groups * width
    assert file_rows.shape[1] == L

    vmem = pl.BlockSpec(memory_space=pltpu.VMEM)
    hbm = pl.BlockSpec(memory_space=pltpu.HBM)
    given = (
        filter_taps.reshape(1, TAPS),
        source_channels,
        channel_list.reshape(1, -1),
        file_rows,
        jnp.asarray(quarter_table()),
        jnp.asarray(inverse_table()),
    )
    chan_spec, src_spec, inverse = pl.pallas_call(
        functools.partial(spectra_kernel, (chan_count, wins, cores)),
        in_specs=[hbm] * 6,
        out_specs=[vmem] * 3,
        out_shape=[
            pltpu.VMEM((channels, wins * 2 * FB), jnp.float32),
            pltpu.VMEM((sources, wins * 2 * FB), jnp.bfloat16),
            pltpu.VMEM((2 * FB, LAGS), jnp.bfloat16),
        ],
        scratch_shapes=[
            pltpu.VMEM((1, TAPS), jnp.bfloat16),
            pltpu.VMEM((groups, width), jnp.int32),
            pltpu.VMEM((1, channel_list.shape[0]), jnp.int32),
            pltpu.VMEM((share, L), jnp.bfloat16),
            pltpu.VMEM((L // CHUNK * share, CHUNK), jnp.float32),
            pltpu.VMEM((L // CHUNK * share, CHUNK), jnp.bfloat16),
            pltpu.VMEM((FOLD * share, L // FOLD), jnp.bfloat16),
            pltpu.VMEM((384, 256), jnp.bfloat16),
            pltpu.VMEM((1, 256), jnp.float32),
            pltpu.VMEM((L // FOLD, 2 * FB), jnp.bfloat16),
            pltpu.VMEM((wins, chan_count, count, 2 * FB), jnp.bfloat16),
            pltpu.VMEM((chan_count, 1, -(-count // 128) * 128), jnp.int32),
            pltpu.SemaphoreType.DMA((6,)),
            pltpu.SemaphoreType.DMA((chan_count, wins, cores)),
            pltpu.SemaphoreType.DMA((chan_count, wins, cores)),
            pltpu.SemaphoreType.DMA((2, chan_count)),
        ],
        compiler_params=pltpu.CompilerParams(
            collective_id=0, has_side_effects=True, vmem_limit_bytes=SPECTRA_VMEM
        ),
        name="spectra",
    )(*(pltpu.with_memory_space_constraint(array, pltpu.HBM) for array in given))

    step = min(4, channels)
    steps = (step,) * (channels // step)
    return pl.pallas_call(
        functools.partial(correlate_kernel, wins, steps),
        in_specs=[vmem, vmem, vmem],
        out_specs=pl.BlockSpec(memory_space=pl.ANY),
        out_shape=jax.ShapeDtypeStruct((channels, sources, LAGS), jnp.float32),
        scratch_shapes=[
            pltpu.VMEM((channels, sources, LAGS), jnp.float32),
            pltpu.SemaphoreType.DMA((len(steps),)),
        ],
        compiler_params=pltpu.CompilerParams(vmem_limit_bytes=CORRELATE_VMEM),
        name="correlate",
    )(inverse, src_spec, chan_spec)


def solution(mesh):
    placed = (P(("fibre", "chan"), "win"), P(("fibre", "chan")), P(), P(("fibre", "grp"), None))
    return jax.shard_map(
        local,
        mesh=mesh,
        in_specs=placed,
        out_specs=P(("fibre", "chan", "win"), "grp", None),
        check_vma=False,
    )
```

```python
import functools
import math

import jax
import jax.numpy as jnp
import ml_dtypes
import numpy as np
from jax import lax
from jax.experimental import pallas as pl
from jax.experimental.pallas import tpu as pltpu
from jax.sharding import PartitionSpec as P

L = 4096
FB = 256
F0 = 8
LAGS = 256
TAPS = 64
HALF = 64
SMOOTH = 8
CH_DEV = 128
FOLD = 4
CHUNK = 256
SPECTRA_VMEM = 52 * 1024 * 1024
CORRELATE_VMEM = 40 * 1024 * 1024

epsilon = 1e-06
water_level = 0.1


def quarter_table():
    samples = np.arange(L // FOLD)
    bins = np.arange(FB) + F0
    phase = np.mod(samples[:, None] * bins[None, :], L) * (2.0 * math.pi / L)
    table = np.concatenate([np.cos(phase), -np.sin(phase)], axis=1)
    return table.astype(np.float32).astype(ml_dtypes.bfloat16)


def inverse_table():
    bins = np.arange(FB) + F0
    shifts = np.arange(LAGS) - LAGS // 2
    turn = np.mod(bins[:, None] * shifts[None, :], L).astype(np.float32) * np.float32(2.0 * math.pi / L)
    inverse = np.concatenate([np.cos(turn), -np.sin(turn)], axis=0) / math.sqrt(FB)
    return inverse.astype(ml_dtypes.bfloat16)


def dot(a, b):
    return jnp.dot(a, b, preferred_element_type=jnp.float32)


def iota(shape, axis):
    return lax.broadcasted_iota(jnp.int32, shape, axis)


def other(index, step):
    for bit in range(step.bit_length()):
        if (step >> bit) & 1:
            index = index + 2**bit - 2 ** (bit + 1) * ((index // 2**bit) % 2)
    return index


def build_toeplitz(taps_ref, wide_taps, toeplitz):
    wide_taps[...] = jnp.zeros_like(wide_taps)
    wide_taps[:, :TAPS] = taps_ref[...].astype(jnp.float32)
    moved = jnp.broadcast_to(wide_taps[...], (128, 256))
    row = iota((128, 256), 0)
    for bit in range(7):
        moved = jnp.where((row >> bit) & 1 == 1, pltpu.roll(moved, 2**bit, 1), moved)
    moved = moved.astype(jnp.bfloat16)
    here, before = moved[:, :128], moved[:, 128:]
    zero = jnp.zeros((128, 128), jnp.bfloat16)
    toeplitz[0:128, :] = jnp.concatenate([before, zero], axis=1)
    toeplitz[128:256, :] = jnp.concatenate([here, before], axis=1)
    toeplitz[256:384, :] = jnp.concatenate([zero, here], axis=1)


def whiten_rows(rows_ref, toeplitz, filt, size, normed, table, table_ready):
    count = rows_ref.shape[0]
    blocks = L // CHUNK
    group = 4
    zero = jnp.zeros((count, 128), jnp.bfloat16)
    for g in range(0, blocks, group):
        parts = [
            rows_ref[:, j * CHUNK - 128 : (j + 1) * CHUNK]
            if j
            else jnp.concatenate([zero, rows_ref[:, :CHUNK]], axis=1)
            for j in range(g, g + group)
        ]
        part = dot(jnp.concatenate(parts, axis=0), toeplitz[...])
        filt[g * count : (g + group) * count, :] = part
        size[g * count : (g + group) * count, :] = jnp.abs(part).astype(jnp.bfloat16)

    reach = jnp.abs(iota((512, CHUNK), 0) - 128 - iota((512, CHUNK), 1)) <= HALF
    band = reach.astype(jnp.float32).astype(jnp.bfloat16)
    for g in range(0, blocks, group):
        parts = []
        for j in range(g, g + group):
            low = size[(j - 1) * count : j * count, 128:] if j else zero
            high = size[(j + 1) * count : (j + 2) * count, :128] if j < blocks - 1 else zero
            parts.append(jnp.concatenate([low, size[j * count : (j + 1) * count, :], high], axis=1))
        total = dot(jnp.concatenate(parts, axis=0), band)
        for j in range(g, g + group):
            position = j * CHUNK + iota((1, CHUNK), 1)
            width = jnp.minimum(position, HALF) + jnp.minimum(L - 1 - position, HALF) + 1
            scale = 1.0 / width.astype(jnp.float32)
            fold, at = divmod(j * CHUNK, L // FOLD)
            normed[fold * count : (fold + 1) * count, at : at + CHUNK] = (
                filt[j * count : (j + 1) * count, :]
                / (total[(j - g) * count : (j - g + 1) * count] * scale + epsilon)
            ).astype(jnp.bfloat16)

    table_ready()
    quarters = dot(normed[...], table[...])
    k = iota((1, FB), 1) + F0
    real = imag = jnp.zeros((count, FB), jnp.float32)
    for fold in range(FOLD):
        turns = (k * fold) % 4
        cosine = jnp.where(turns == 0, 1.0, jnp.where(turns == 2, -1.0, 0.0))
        sine = jnp.where(turns == 1, 1.0, jnp.where(turns == 3, -1.0, 0.0))
        re = quarters[fold * count : (fold + 1) * count, :FB]
        im = quarters[fold * count : (fold + 1) * count, FB:]
        real = real + cosine * re + sine * im
        imag = imag + cosine * im - sine * re
    energy = real * real + imag * imag
    near = jnp.abs(iota((FB, FB), 0) - iota((FB, FB), 1)) <= SMOOTH
    near = near.astype(jnp.float32).astype(jnp.bfloat16)
    upper = energy.astype(jnp.bfloat16)
    left = energy - upper.astype(jnp.float32)
    middle = left.astype(jnp.bfloat16)
    lower = (left - middle.astype(jnp.float32)).astype(jnp.bfloat16)
    split = dot(jnp.concatenate([upper, middle, lower], axis=0), near)
    total = split[:count] + split[count : 2 * count] + split[2 * count :]
    k = iota((1, FB), 1)
    width = jnp.minimum(k, SMOOTH) + jnp.minimum(FB - 1 - k, SMOOTH) + 1
    smooth = total / width.astype(jnp.float32)
    level = jnp.sum(energy, axis=1, keepdims=True) * (1.0 / FB)
    factor = lax.rsqrt(smooth + water_level * level + epsilon)
    return real * factor, imag * factor


def spectra_kernel(sizes, taps_hbm, sources_hbm, label_hbm, file_ref, table_ref, turn_ref, chan_ref, src_ref, inverse_ref,
                   taps_ref, sources_ref, label_ref, rows, filt, size, normed, toeplitz, wide_taps, table, held, labels,
                   load_sems, send_sems, recv_sems, label_sems):
    zs, xs, cs = sizes
    z, x, c = lax.axis_index("chan"), lax.axis_index("win"), lax.axis_index("grp")
    share = rows.shape[0]
    count = share * cs
    own = pl.ds(pl.multiple_of(c * share, share), share)

    small = []
    for source, target in ((taps_hbm, taps_ref), (label_hbm, label_ref), (sources_hbm, sources_ref)):
        copy = pltpu.make_async_copy(source, target, load_sems.at[3 + len(small)])
        copy.start()
        small.append(copy)
    fetch = pltpu.make_async_copy(file_ref.at[own, :], rows, load_sems.at[0])
    fetch.start()
    load = pltpu.make_async_copy(table_ref, table, load_sems.at[1])
    load.start()
    turn = pltpu.make_async_copy(turn_ref, inverse_ref, load_sems.at[2])

    barrier = pltpu.get_barrier_semaphore()
    swap = 1 if cs > 1 else 0
    partners = [{"chan": other(z, d), "grp": other(c, swap)} for d in range(1, zs)]
    partners += [{"win": other(x, e), "grp": other(c, swap)} for e in range(1, xs)]
    partners += [{"grp": other(c, f)} for f in range(1, cs)]
    for partner in partners:
        pl.semaphore_signal(barrier, inc=1, device_id=partner, device_id_type=pl.DeviceIdType.MESH)

    labels[0] = jnp.zeros(labels.shape[1:], jnp.int32)
    for copy in small:
        copy.wait()
    labels[0, :, :count] = label_ref[:, :count]
    build_toeplitz(taps_ref, wide_taps, toeplitz)
    fetch.wait()
    real, imag = whiten_rows(rows, toeplitz, filt, size, normed, table, load.wait)
    held[0, 0, own, :FB] = real.astype(jnp.bfloat16)
    held[0, 0, own, FB:] = imag.astype(jnp.bfloat16)

    pl.semaphore_wait(barrier, len(partners))

    copies = {}

    def send(d, e, f, source, target, mine):
        copy = pltpu.make_async_remote_copy(
            src_ref=held.at[source[1], source[0], mine],
            dst_ref=held.at[e, d, mine],
            send_sem=send_sems.at[d, e, f],
            recv_sem=recv_sems.at[d, e, f],
            device_id=target,
            device_id_type=pl.DeviceIdType.MESH,
        )
        copy.start()
        copies[d, e, f] = copy

    def along_win(d):
        for e in range(1, xs):
            send(d, e, 0, (d, 0), {"win": other(x, e), "grp": other(c, swap)}, brought(d, 0))

    def along_chan(d, e):
        send(d, e, 0, (0, e), {"chan": other(z, d), "grp": other(c, swap)}, brought(0, e))

    def along_grp(d, e):
        for f in range(1, cs):
            send(d, e, f, (d, e), {"grp": other(c, f)}, brought(d, e))

    def brought(d, e):
        core = other(c, swap * (((d > 0) + (e > 0)) % 2))
        return pl.ds(pl.multiple_of(core * share, share), share)

    across = zs - 1
    told = []
    for d in range(1, zs):
        copy = pltpu.make_async_remote_copy(
            src_ref=labels.at[0],
            dst_ref=labels.at[d],
            send_sem=label_sems.at[0, d],
            recv_sem=label_sems.at[1, d],
            device_id={"chan": other(z, d), "grp": other(c, swap)},
            device_id_type=pl.DeviceIdType.MESH,
        )
        copy.start()
        told.append(copy)
    along_win(0)
    for d in range(1, zs):
        along_chan(d, 0)
    along_grp(0, 0)

    turn.start()

    groups, width = sources_ref.shape
    channels = chan_ref.shape[0]
    diagonal = iota((width, width), 0) == iota((width, width), 1)
    wanted = [
        jnp.sum(jnp.where(diagonal, sources_ref[g : g + 1, :], 0), axis=1, keepdims=True)
        for g in range(groups)
    ]
    wanted.append(z * CH_DEV + x * channels + iota((channels, 1), 0))
    wanted = jnp.concatenate(wanted, axis=0)

    for d in range(1, across):
        copies[d, 0, 0].wait_recv()
        along_win(d)
        along_grp(d, 0)
    for e in range(1, xs):
        copies[0, e, 0].wait_recv()
        if across:
            along_chan(across, e)
        along_grp(0, e)
    if across:
        copies[across, 0, 0].wait_recv()
        along_grp(across, 0)

    for copy in told:
        copy.wait()
    span = max(1, 2 * FB // count)
    picks = []
    for d in range(0, zs, span):
        names = jnp.concatenate([labels[d + i, :, :count] for i in range(min(span, zs - d))], axis=1)
        picks.append((wanted == names).astype(jnp.float32).astype(jnp.bfloat16))

    def select(e):
        total = None
        for d, pick in zip(range(0, zs, span), picks):
            block = held[e, d : d + span]
            part = dot(pick, block.reshape(block.shape[0] * count, 2 * FB))
            total = part if total is None else total + part
        at = e * 2 * FB
        src_ref[:, at : at + 2 * FB] = total[: groups * width].astype(jnp.bfloat16)
        chan_ref[:, at : at + 2 * FB] = total[groups * width :]

    for e in range(1, xs):
        for d in range(1, zs):
            copies[d, e, 0].wait_recv()
            along_grp(d, e)
    for d in range(zs):
        for f in range(1, cs):
            copies[d, 0, f].wait_recv()
    select(0)
    for e in range(1, xs):
        for d in range(zs):
            for f in range(1, cs):
                copies[d, e, f].wait_recv()
        select(e)
    for copy in copies.values():
        copy.wait_send()
    turn.wait()


def correlate_kernel(wins, steps, inverse_ref, src_ref, chan_ref, out_ref, made, sems):
    inverse = inverse_ref[...]
    copies = []
    begin = 0
    for step in steps:
        pair = 2 if step % 2 == 0 else 1
        for first in range(begin, begin + step, pair):
            cross = []
            for c in range(first, first + pair):
                real = imag = None
                for w in range(wins):
                    at = w * 2 * FB
                    p, q = src_ref[:, at : at + FB], src_ref[:, at + FB : at + 2 * FB]
                    row = chan_ref[c : c + 1, at : at + 2 * FB].astype(jnp.bfloat16)
                    a, b = row[:, :FB], row[:, FB:]
                    re, im = a * p + b * q, b * p - a * q
                    real = re if real is None else real + re
                    imag = im if imag is None else imag + im
                cross.append(jnp.concatenate([real, imag], axis=1))
            result = dot(jnp.concatenate(cross, axis=0), inverse)
            made[first : first + pair] = result.reshape(pair, *made.shape[1:])
        part = pl.ds(begin, step)
        copy = pltpu.make_async_copy(made.at[part], out_ref.at[part], sems.at[len(copies)])
        copy.start()
        copies.append(copy)
        begin += step
    for copy in copies:
        copy.wait()


def local(file_rows, channel_list, filter_taps, source_channels):
    chan_count = lax.axis_size("chan")
    wins = lax.axis_size("win")
    cores = lax.axis_size("grp")
    count = chan_count * (CH_DEV // 4)
    share = count // cores
    channels = CH_DEV // wins
    groups, width = source_channels.shape
    sources = groups * width
    assert file_rows.shape[1] == L

    vmem = pl.BlockSpec(memory_space=pltpu.VMEM)
    hbm = pl.BlockSpec(memory_space=pltpu.HBM)
    given = (
        filter_taps.reshape(1, TAPS),
        source_channels,
        channel_list.reshape(1, -1),
        file_rows,
        jnp.asarray(quarter_table()),
        jnp.asarray(inverse_table()),
    )
    chan_spec, src_spec, inverse = pl.pallas_call(
        functools.partial(spectra_kernel, (chan_count, wins, cores)),
        in_specs=[hbm] * 6,
        out_specs=[vmem] * 3,
        out_shape=[
            pltpu.VMEM((channels, wins * 2 * FB), jnp.float32),
            pltpu.VMEM((sources, wins * 2 * FB), jnp.bfloat16),
            pltpu.VMEM((2 * FB, LAGS), jnp.bfloat16),
        ],
        scratch_shapes=[
            pltpu.VMEM((1, TAPS), jnp.bfloat16),
            pltpu.VMEM((groups, width), jnp.int32),
            pltpu.VMEM((1, channel_list.shape[0]), jnp.int32),
            pltpu.VMEM((share, L), jnp.bfloat16),
            pltpu.VMEM((L // CHUNK * share, CHUNK), jnp.float32),
            pltpu.VMEM((L // CHUNK * share, CHUNK), jnp.bfloat16),
            pltpu.VMEM((FOLD * share, L // FOLD), jnp.bfloat16),
            pltpu.VMEM((384, 256), jnp.bfloat16),
            pltpu.VMEM((1, 256), jnp.float32),
            pltpu.VMEM((L // FOLD, 2 * FB), jnp.bfloat16),
            pltpu.VMEM((wins, chan_count, count, 2 * FB), jnp.bfloat16),
            pltpu.VMEM((chan_count, 1, -(-count // 128) * 128), jnp.int32),
            pltpu.SemaphoreType.DMA((6,)),
            pltpu.SemaphoreType.DMA((chan_count, wins, cores)),
            pltpu.SemaphoreType.DMA((chan_count, wins, cores)),
            pltpu.SemaphoreType.DMA((2, chan_count)),
        ],
        compiler_params=pltpu.CompilerParams(
            collective_id=0, has_side_effects=True, vmem_limit_bytes=SPECTRA_VMEM
        ),
        name="spectra",
    )(*(pltpu.with_memory_space_constraint(array, pltpu.HBM) for array in given))

    step = min(4, channels)
    steps = (step,) * (channels // step)
    return pl.pallas_call(
        functools.partial(correlate_kernel, wins, steps),
        in_specs=[vmem, vmem, vmem],
        out_specs=pl.BlockSpec(memory_space=pl.ANY),
        out_shape=jax.ShapeDtypeStruct((channels, sources, LAGS), jnp.float32),
        scratch_shapes=[
            pltpu.VMEM((channels, sources, LAGS), jnp.float32),
            pltpu.SemaphoreType.DMA((len(steps),)),
        ],
        compiler_params=pltpu.CompilerParams(vmem_limit_bytes=CORRELATE_VMEM),
        name="correlate",
    )(inverse, src_spec, chan_spec)


def solution(mesh):
    placed = (P(("fibre", "chan"), "win"), P(("fibre", "chan")), P(), P(("fibre", "grp"), None))
    return jax.shard_map(
        local,
        mesh=mesh,
        in_specs=placed,
        out_specs=P(("fibre", "chan", "win"), "grp", None),
        check_vma=False,
    )
```

```python
import functools
import math

import jax
import jax.numpy as jnp
import ml_dtypes
import numpy as np
from jax import lax
from jax.experimental import pallas as pl
from jax.experimental.pallas import tpu as pltpu
from jax.sharding import PartitionSpec as P

L = 4096
FB = 256
F0 = 8
LAGS = 256
TAPS = 64
HALF = 64
SMOOTH = 8
CH_DEV = 128
FOLD = 4
CHUNK = 256
SPECTRA_VMEM = 52 * 1024 * 1024
CORRELATE_VMEM = 40 * 1024 * 1024

epsilon = 1e-06
water_level = 0.1


def quarter_table():
    samples = np.arange(L // FOLD)
    bins = np.arange(FB) + F0
    phase = np.mod(samples[:, None] * bins[None, :], L) * (2.0 * math.pi / L)
    table = np.concatenate([np.cos(phase), -np.sin(phase)], axis=1)
    return table.astype(np.float32).astype(ml_dtypes.bfloat16)


def inverse_table():
    bins = np.arange(FB) + F0
    shifts = np.arange(LAGS) - LAGS // 2
    turn = np.mod(bins[:, None] * shifts[None, :], L).astype(np.float32) * np.float32(2.0 * math.pi / L)
    inverse = np.concatenate([np.cos(turn), -np.sin(turn)], axis=0) / math.sqrt(FB)
    return inverse.astype(ml_dtypes.bfloat16)


def dot(a, b):
    return jnp.dot(a, b, preferred_element_type=jnp.float32)


def iota(shape, axis):
    return lax.broadcasted_iota(jnp.int32, shape, axis)


def other(index, step):
    for bit in range(step.bit_length()):
        if (step >> bit) & 1:
            index = index + 2**bit - 2 ** (bit + 1) * ((index // 2**bit) % 2)
    return index


def build_toeplitz(taps_ref, wide_taps, toeplitz):
    wide_taps[...] = jnp.zeros_like(wide_taps)
    wide_taps[:, :TAPS] = taps_ref[...].astype(jnp.float32)
    moved = jnp.broadcast_to(wide_taps[...], (128, 256))
    row = iota((128, 256), 0)
    for bit in range(7):
        moved = jnp.where((row >> bit) & 1 == 1, pltpu.roll(moved, 2**bit, 1), moved)
    moved = moved.astype(jnp.bfloat16)
    here, before = moved[:, :128], moved[:, 128:]
    zero = jnp.zeros((128, 128), jnp.bfloat16)
    toeplitz[0:128, :] = jnp.concatenate([before, zero], axis=1)
    toeplitz[128:256, :] = jnp.concatenate([here, before], axis=1)
    toeplitz[256:384, :] = jnp.concatenate([zero, here], axis=1)


def whiten_rows(rows_ref, toeplitz, filt, size, normed, table, table_ready):
    count = rows_ref.shape[0]
    blocks = L // CHUNK
    group = 4
    zero = jnp.zeros((count, 128), jnp.bfloat16)
    for g in range(0, blocks, group):
        parts = [
            rows_ref[:, j * CHUNK - 128 : (j + 1) * CHUNK]
            if j
            else jnp.concatenate([zero, rows_ref[:, :CHUNK]], axis=1)
            for j in range(g, g + group)
        ]
        part = dot(jnp.concatenate(parts, axis=0), toeplitz[...])
        filt[g * count : (g + group) * count, :] = part
        size[g * count : (g + group) * count, :] = jnp.abs(part).astype(jnp.bfloat16)

    reach = jnp.abs(iota((512, CHUNK), 0) - 128 - iota((512, CHUNK), 1)) <= HALF
    band = reach.astype(jnp.float32).astype(jnp.bfloat16)
    for g in range(0, blocks, group):
        parts = []
        for j in range(g, g + group):
            low = size[(j - 1) * count : j * count, 128:] if j else zero
            high = size[(j + 1) * count : (j + 2) * count, :128] if j < blocks - 1 else zero
            parts.append(jnp.concatenate([low, size[j * count : (j + 1) * count, :], high], axis=1))
        total = dot(jnp.concatenate(parts, axis=0), band)
        for j in range(g, g + group):
            position = j * CHUNK + iota((1, CHUNK), 1)
            width = jnp.minimum(position, HALF) + jnp.minimum(L - 1 - position, HALF) + 1
            scale = 1.0 / width.astype(jnp.float32)
            fold, at = divmod(j * CHUNK, L // FOLD)
            normed[fold * count : (fold + 1) * count, at : at + CHUNK] = (
                filt[j * count : (j + 1) * count, :]
                / (total[(j - g) * count : (j - g + 1) * count] * scale + epsilon)
            ).astype(jnp.bfloat16)

    table_ready()
    quarters = dot(normed[...], table[...])
    k = iota((1, FB), 1) + F0
    real = imag = jnp.zeros((count, FB), jnp.float32)
    for fold in range(FOLD):
        turns = (k * fold) % 4
        cosine = jnp.where(turns == 0, 1.0, jnp.where(turns == 2, -1.0, 0.0))
        sine = jnp.where(turns == 1, 1.0, jnp.where(turns == 3, -1.0, 0.0))
        re = quarters[fold * count : (fold + 1) * count, :FB]
        im = quarters[fold * count : (fold + 1) * count, FB:]
        real = real + cosine * re + sine * im
        imag = imag + cosine * im - sine * re
    energy = real * real + imag * imag
    near = jnp.abs(iota((FB, FB), 0) - iota((FB, FB), 1)) <= SMOOTH
    near = near.astype(jnp.float32).astype(jnp.bfloat16)
    upper = energy.astype(jnp.bfloat16)
    left = energy - upper.astype(jnp.float32)
    middle = left.astype(jnp.bfloat16)
    lower = (left - middle.astype(jnp.float32)).astype(jnp.bfloat16)
    split = dot(jnp.concatenate([upper, middle, lower], axis=0), near)
    total = split[:count] + split[count : 2 * count] + split[2 * count :]
    k = iota((1, FB), 1)
    width = jnp.minimum(k, SMOOTH) + jnp.minimum(FB - 1 - k, SMOOTH) + 1
    smooth = total / width.astype(jnp.float32)
    level = jnp.sum(energy, axis=1, keepdims=True) * (1.0 / FB)
    factor = lax.rsqrt(smooth + water_level * level + epsilon)
    return real * factor, imag * factor


def spectra_kernel(sizes, taps_hbm, sources_hbm, label_hbm, file_ref, table_ref, turn_ref, chan_ref, src_ref, inverse_ref,
                   taps_ref, sources_ref, label_ref, rows, filt, size, normed, toeplitz, wide_taps, table, held, labels,
                   load_sems, send_sems, recv_sems, label_sems):
    zs, xs, cs = sizes
    z, x, c = lax.axis_index("chan"), lax.axis_index("win"), lax.axis_index("grp")
    share = rows.shape[0]
    count = share * cs
    own = pl.ds(pl.multiple_of(c * share, share), share)

    small = []
    for source, target in ((taps_hbm, taps_ref), (label_hbm, label_ref), (sources_hbm, sources_ref)):
        copy = pltpu.make_async_copy(source, target, load_sems.at[3 + len(small)])
        copy.start()
        small.append(copy)
    fetch = pltpu.make_async_copy(file_ref.at[own, :], rows, load_sems.at[0])
    fetch.start()
    load = pltpu.make_async_copy(table_ref, table, load_sems.at[1])
    load.start()
    turn = pltpu.make_async_copy(turn_ref, inverse_ref, load_sems.at[2])

    barrier = pltpu.get_barrier_semaphore()
    swap = 1 if cs > 1 else 0
    partners = [{"chan": other(z, d), "grp": other(c, swap)} for d in range(1, zs)]
    partners += [{"win": other(x, e), "grp": other(c, swap)} for e in range(1, xs)]
    partners += [{"grp": other(c, f)} for f in range(1, cs)]
    for partner in partners:
        pl.semaphore_signal(barrier, inc=1, device_id=partner, device_id_type=pl.DeviceIdType.MESH)

    labels[0] = jnp.zeros(labels.shape[1:], jnp.int32)
    for copy in small:
        copy.wait()
    labels[0, :, :count] = label_ref[:, :count]
    build_toeplitz(taps_ref, wide_taps, toeplitz)
    fetch.wait()
    real, imag = whiten_rows(rows, toeplitz, filt, size, normed, table, load.wait)
    held[0, 0, own, :FB] = real.astype(jnp.bfloat16)
    held[0, 0, own, FB:] = imag.astype(jnp.bfloat16)

    pl.semaphore_wait(barrier, len(partners))

    copies = {}

    def send(d, e, f, source, target, mine):
        copy = pltpu.make_async_remote_copy(
            src_ref=held.at[source[1], source[0], mine],
            dst_ref=held.at[e, d, mine],
            send_sem=send_sems.at[d, e, f],
            recv_sem=recv_sems.at[d, e, f],
            device_id=target,
            device_id_type=pl.DeviceIdType.MESH,
        )
        copy.start()
        copies[d, e, f] = copy

    def along_win(d):
        for e in range(1, xs):
            send(d, e, 0, (d, 0), {"win": other(x, e), "grp": other(c, swap)}, brought(d, 0))

    def along_chan(d, e):
        send(d, e, 0, (0, e), {"chan": other(z, d), "grp": other(c, swap)}, brought(0, e))

    def along_grp(d, e):
        for f in range(1, cs):
            send(d, e, f, (d, e), {"grp": other(c, f)}, brought(d, e))

    def brought(d, e):
        core = other(c, swap * (((d > 0) + (e > 0)) % 2))
        return pl.ds(pl.multiple_of(core * share, share), share)

    across = zs - 1
    told = []
    for d in range(1, zs):
        copy = pltpu.make_async_remote_copy(
            src_ref=labels.at[0],
            dst_ref=labels.at[d],
            send_sem=label_sems.at[0, d],
            recv_sem=label_sems.at[1, d],
            device_id={"chan": other(z, d), "grp": other(c, swap)},
            device_id_type=pl.DeviceIdType.MESH,
        )
        copy.start()
        told.append(copy)
    along_win(0)
    for d in range(1, zs):
        along_chan(d, 0)
    along_grp(0, 0)

    turn.start()

    groups, width = sources_ref.shape
    channels = chan_ref.shape[0]
    diagonal = iota((width, width), 0) == iota((width, width), 1)
    wanted = [
        jnp.sum(jnp.where(diagonal, sources_ref[g : g + 1, :], 0), axis=1, keepdims=True)
        for g in range(groups)
    ]
    wanted.append(z * CH_DEV + x * channels + iota((channels, 1), 0))
    wanted = jnp.concatenate(wanted, axis=0)

    for d in range(1, across):
        copies[d, 0, 0].wait_recv()
        along_win(d)
        along_grp(d, 0)
    for e in range(1, xs):
        copies[0, e, 0].wait_recv()
        if across:
            along_chan(across, e)
        along_grp(0, e)
    if across:
        copies[across, 0, 0].wait_recv()
        along_grp(across, 0)

    for copy in told:
        copy.wait()
    span = max(1, 2 * FB // count)
    picks = []
    for d in range(0, zs, span):
        names = jnp.concatenate([labels[d + i, :, :count] for i in range(min(span, zs - d))], axis=1)
        picks.append((wanted == names).astype(jnp.float32).astype(jnp.bfloat16))

    def select(e):
        total = None
        for d, pick in zip(range(0, zs, span), picks):
            block = held[e, d : d + span]
            part = dot(pick, block.reshape(block.shape[0] * count, 2 * FB))
            total = part if total is None else total + part
        at = e * 2 * FB
        src_ref[:, at : at + 2 * FB] = total[: groups * width].astype(jnp.bfloat16)
        chan_ref[:, at : at + 2 * FB] = total[groups * width :]

    for e in range(1, xs):
        for d in range(1, zs):
            copies[d, e, 0].wait_recv()
            along_grp(d, e)
    for d in range(zs):
        for f in range(1, cs):
            copies[d, 0, f].wait_recv()
    select(0)
    turn.wait()
    last = [copies.pop((across, e, f)) for e in range(1, xs) for f in range(1, cs)]
    for copy in copies.values():
        copy.wait_send()
    for e in range(1, xs):
        for f in range(1, cs):
            for d in range(across):
                copies[d, e, f].wait_recv()
    for copy in last:
        copy.wait_recv()
    for e in range(1, xs):
        select(e)
    for copy in last:
        copy.wait_send()


def correlate_kernel(wins, steps, inverse_ref, src_ref, chan_ref, out_ref, made, sems):
    inverse = inverse_ref[...]
    copies = []
    begin = 0
    for step in steps:
        pair = 2 if step % 2 == 0 else 1
        for first in range(begin, begin + step, pair):
            cross = []
            for c in range(first, first + pair):
                real = imag = None
                for w in range(wins):
                    at = w * 2 * FB
                    p, q = src_ref[:, at : at + FB], src_ref[:, at + FB : at + 2 * FB]
                    row = chan_ref[c : c + 1, at : at + 2 * FB].astype(jnp.bfloat16)
                    a, b = row[:, :FB], row[:, FB:]
                    re, im = a * p + b * q, b * p - a * q
                    real = re if real is None else real + re
                    imag = im if imag is None else imag + im
                cross.append(jnp.concatenate([real, imag], axis=1))
            result = dot(jnp.concatenate(cross, axis=0), inverse)
            made[first : first + pair] = result.reshape(pair, *made.shape[1:])
        part = pl.ds(begin, step)
        copy = pltpu.make_async_copy(made.at[part], out_ref.at[part], sems.at[len(copies)])
        copy.start()
        copies.append(copy)
        begin += step
    for copy in copies:
        copy.wait()


def local(file_rows, channel_list, filter_taps, source_channels):
    chan_count = lax.axis_size("chan")
    wins = lax.axis_size("win")
    cores = lax.axis_size("grp")
    count = chan_count * (CH_DEV // 4)
    share = count // cores
    channels = CH_DEV // wins
    groups, width = source_channels.shape
    sources = groups * width
    assert file_rows.shape[1] == L

    vmem = pl.BlockSpec(memory_space=pltpu.VMEM)
    hbm = pl.BlockSpec(memory_space=pltpu.HBM)
    given = (
        filter_taps.reshape(1, TAPS),
        source_channels,
        channel_list.reshape(1, -1),
        file_rows,
        jnp.asarray(quarter_table()),
        jnp.asarray(inverse_table()),
    )
    chan_spec, src_spec, inverse = pl.pallas_call(
        functools.partial(spectra_kernel, (chan_count, wins, cores)),
        in_specs=[hbm] * 6,
        out_specs=[vmem] * 3,
        out_shape=[
            pltpu.VMEM((channels, wins * 2 * FB), jnp.float32),
            pltpu.VMEM((sources, wins * 2 * FB), jnp.bfloat16),
            pltpu.VMEM((2 * FB, LAGS), jnp.bfloat16),
        ],
        scratch_shapes=[
            pltpu.VMEM((1, TAPS), jnp.bfloat16),
            pltpu.VMEM((groups, width), jnp.int32),
            pltpu.VMEM((1, channel_list.shape[0]), jnp.int32),
            pltpu.VMEM((share, L), jnp.bfloat16),
            pltpu.VMEM((L // CHUNK * share, CHUNK), jnp.float32),
            pltpu.VMEM((L // CHUNK * share, CHUNK), jnp.bfloat16),
            pltpu.VMEM((FOLD * share, L // FOLD), jnp.bfloat16),
            pltpu.VMEM((384, 256), jnp.bfloat16),
            pltpu.VMEM((1, 256), jnp.float32),
            pltpu.VMEM((L // FOLD, 2 * FB), jnp.bfloat16),
            pltpu.VMEM((wins, chan_count, count, 2 * FB), jnp.bfloat16),
            pltpu.VMEM((chan_count, 1, -(-count // 128) * 128), jnp.int32),
            pltpu.SemaphoreType.DMA((6,)),
            pltpu.SemaphoreType.DMA((chan_count, wins, cores)),
            pltpu.SemaphoreType.DMA((chan_count, wins, cores)),
            pltpu.SemaphoreType.DMA((2, chan_count)),
        ],
        compiler_params=pltpu.CompilerParams(
            collective_id=0, has_side_effects=True, vmem_limit_bytes=SPECTRA_VMEM
        ),
        name="spectra",
    )(*(pltpu.with_memory_space_constraint(array, pltpu.HBM) for array in given))

    step = min(4, channels)
    steps = (step,) * (channels // step)
    return pl.pallas_call(
        functools.partial(correlate_kernel, wins, steps),
        in_specs=[vmem, vmem, vmem],
        out_specs=pl.BlockSpec(memory_space=pl.ANY),
        out_shape=jax.ShapeDtypeStruct((channels, sources, LAGS), jnp.float32),
        scratch_shapes=[
            pltpu.VMEM((channels, sources, LAGS), jnp.float32),
            pltpu.SemaphoreType.DMA((len(steps),)),
        ],
        compiler_params=pltpu.CompilerParams(vmem_limit_bytes=CORRELATE_VMEM),
        name="correlate",
    )(inverse, src_spec, chan_spec)


def solution(mesh):
    placed = (P(("fibre", "chan"), "win"), P(("fibre", "chan")), P(), P(("fibre", "grp"), None))
    return jax.shard_map(
        local,
        mesh=mesh,
        in_specs=placed,
        out_specs=P(("fibre", "chan", "win"), "grp", None),
        check_vma=False,
    )
```
